256 devices in a mesh: axial: 16 (over x, z_hi, core), radial: 4 (over y), pitch: 4 (over z_lo).
Axes of the slice: x: 4, y: 4, z: 8 (z_hi: 2, z_lo: 4; z = z_hi * 4 + z_lo), core: 2. Of those that a mesh axis runs over, the one named last changes fastest.
Arguments:
- rhs: float32 [2, 5, 128, 64, 512], P(None, None, 'axial', 'radial', 'pitch'), may hold values from -12 to 12
- jac0: float32 [5, 5, 128, 64, 512], P(None, None, 'axial', 'radial', 'pitch'), may hold values from -1.2 to 9
- shift0: float32 [128, 64, 512], P('axial', 'radial', 'pitch'), may hold values from 0.5 to 3
- jac1: float32 [5, 5, 64, 32, 256], P(None, None, 'axial', 'radial', 'pitch'), may hold values from -1.2 to 9
- shift1: float32 [64, 32, 256], P('axial', 'radial', 'pitch'), may hold values from 0.5 to 3
- jac2: float32 [5, 5, 32, 16, 128], P(None, None, 'axial', 'radial', 'pitch'), may hold values from -1.2 to 9
- shift2: float32 [32, 16, 128], P('axial', 'radial', 'pitch'), may hold values from 0.5 to 3
- blade_mask: int32 [128, 64, 512], P('axial', 'radial', 'pitch'), may hold values 0 or 1
Outputs:
- solution: float32 [2, 5, 128, 64, 512], P(None, None, 'axial', 'radial', 'pitch')
- damping: float32 [], replicated
The draws below stay inside these ranges and needn't reach their ends.
All inputs are finite; a program needn't handle non-finite values. No bound on the sum of `blade_mask` on one device may be relied on, other than what follows from the above.
Results may differ from the reference program's by a relative error of at most 0.025.
Values sent between devices are 32-bit elements; how exact they have to be, the bound alone decides.
A program may use at most 128 MiB of HBM per device.

```python
import math
import jax
import jax.numpy as jnp
from jax import lax

COARSE_SWEEPS = 4
NA = 128
NR = 64
NP = 512


def jacobian_draw(key, spatial):
    key_off, key_diag = jax.random.split(key)
    shape = (5, 5) + spatial
    off_diag = jax.random.uniform(key_off, shape, jnp.float32, -1.2, 1.2)
    diag_vals = jax.random.uniform(key_diag, (5,) + spatial, jnp.float32, 6.0, 9.0)
    eye = jnp.eye(5, dtype=jnp.float32).reshape((5, 5) + (1,) * len(spatial))
    return off_diag * (1.0 - eye) + eye * diag_vals[:, None]


def draw_jac0(key, part):
    return jacobian_draw(jax.random.fold_in(key, 11), (NA, NR, NP))


def draw_jac1(key, part):
    return jacobian_draw(jax.random.fold_in(key, 12), (NA // 2, NR // 2, NP // 2))


def draw_jac2(key, part):
    return jacobian_draw(jax.random.fold_in(key, 13), (NA // 4, NR // 4, NP // 4))


def set_ends(drawn, own_key, least, largest):
    longest = drawn.shape.index(max(drawn.shape))
    spots = []
    for shift in (0, 1):
        where = [jax.random.randint(jax.random.fold_in(own_key, axis), (), 0, length) for axis, length in enumerate(drawn.shape)]
        where[longest] = (where[longest] + shift) % drawn.shape[longest]
        spots.append(tuple(where))
    return drawn.at[spots[0]].set(least).at[spots[1]].set(largest)


def shard_levels(stream_key, shape, pieces, least, high):
    level = 1.0
    for axis_at, blocks in pieces:
        steps = jax.random.uniform(jax.random.fold_in(jax.random.fold_in(stream_key, 6), axis_at), (blocks,), jnp.float32, least / len(pieces), high / len(pieces))
        level = level * jnp.repeat(jnp.exp(steps), shape[axis_at] // blocks).reshape((-1,) + (1,) * (len(shape) - 1 - axis_at))
    return level


def normal_values(key, shape, spread, limit, cuts=(), held_as=jnp.bfloat16):
    array = jax.random.normal(key, shape, jnp.float32) * spread
    if len(cuts) > 0:
        array = shard_levels(key, shape, cuts, -0.22, 0.18) * array
    return jnp.clip(array, min=-limit, max=limit).astype(held_as)


def setup_inputs(seed: int = 0) -> dict:
    splits = jax.random.split(jax.random.key(seed), 9)
    rhs = normal_values(splits[0], (2, 5, NA, NR, NP), 2.0, 12.0, ((2, 16), (3, 4), (4, 4)), jnp.float32)
    jac0 = draw_jac0(jax.random.fold_in(splits[8], 71), 0)
    shift0 = jnp.clip(jnp.exp(math.log(3.0) - 1.7917595 * jax.random.uniform(splits[2], (NA, NR, NP), jnp.float32) ** shard_levels(splits[2], (NA, NR, NP), ((0, 16), (1, 4), (2, 4)), -0.2, 0.2)), 0.5, 3.0)
    jac1 = draw_jac1(jax.random.fold_in(splits[8], 71), 0)
    shift1 = jnp.clip(jnp.exp(math.log(3.0) - 1.7917595 * jax.random.uniform(splits[4], (NA // 2, NR // 2, NP // 2), jnp.float32) ** shard_levels(splits[4], (NA // 2, NR // 2, NP // 2), ((0, 16), (1, 4), (2, 4)), -0.2, 0.2)), 0.5, 3.0)
    jac2 = draw_jac2(jax.random.fold_in(splits[8], 71), 0)
    shift2 = jnp.clip(jnp.exp(math.log(3.0) - 1.7917595 * jax.random.uniform(splits[6], (NA // 4, NR // 4, NP // 4), jnp.float32) ** shard_levels(splits[6], (NA // 4, NR // 4, NP // 4), ((0, 16), (1, 4), (2, 4)), -0.2, 0.2)), 0.5, 3.0)
    blade_mask = set_ends((jax.random.randint(splits[7], (NA, NR, NP), 0, 8) < 1).astype(jnp.int32), jax.random.fold_in(splits[7], 1), 0, 1)
    return {"rhs": rhs, "jac0": jac0, "shift0": shift0, "jac1": jac1, "shift1": shift1, "jac2": jac2, "shift2": shift2, "blade_mask": blade_mask}


def pad_field(field):
    wrapped = jnp.pad(field, ((0, 0), (0, 0), (0, 0), (1, 1)), mode='wrap')
    return jnp.pad(wrapped, ((0, 0), (1, 1), (1, 1), (0, 0)))

def apply_op(padded, jac, shift):
    center = padded[:, 1:-1, 1:-1, 1:-1]
    beside = padded[:, 2:, 1:-1, 1:-1] + padded[:, :-2, 1:-1, 1:-1]
    beside = beside + padded[:, 1:-1, 2:, 1:-1] + padded[:, 1:-1, :-2, 1:-1]
    beside = beside + padded[:, 1:-1, 1:-1, 2:] + padded[:, 1:-1, 1:-1, :-2]
    real_part = center[:5]
    imag_part = center[5:]
    jreal = jnp.einsum('ijarp,jarp->iarp', jac, real_part, precision=lax.Precision.HIGHEST)
    jimag = jnp.einsum('ijarp,jarp->iarp', jac, imag_part, precision=lax.Precision.HIGHEST)
    out_real = jreal - shift * imag_part - beside[:5]
    out_imag = jimag + shift * real_part - beside[5:]
    return jnp.concatenate([out_real, out_imag], 0)

def relax(res, jac, shift):
    diag_entries = jnp.stack([jac[k, k] for k in range(5)])
    denom = diag_entries * diag_entries + shift * shift
    denom = jnp.where(denom > 0, denom, 1.0)
    res_real = res[:5]
    res_imag = res[5:]
    corr_real = (diag_entries * res_real + shift * res_imag) / denom
    corr_imag = (diag_entries * res_imag - shift * res_real) / denom
    return 0.7 * jnp.concatenate([corr_real, corr_imag], 0)

def sweep(field, rhs_level, jac, shift):
    return field + relax(rhs_level - apply_op(pad_field(field), jac, shift), jac, shift)

def residual(field, rhs_level, jac, shift):
    return rhs_level - apply_op(pad_field(field), jac, shift)

def restrict(field):
    k, a, r, p = field.shape
    return lax.optimization_barrier(jnp.mean(field.reshape(k, a // 2, 2, r // 2, 2, p // 2, 2), axis=(2, 4, 6)))

def prolong(field):
    return jnp.repeat(jnp.repeat(jnp.repeat(field, 2, axis=1), 2, axis=2), 2, axis=3)

def reference(rhs, jac0, shift0, jac1, shift1, jac2, shift2, blade_mask):
    fine_rhs = rhs.reshape((10,) + rhs.shape[2:])
    fine = relax(fine_rhs, jac0, shift0)
    fine = sweep(fine, fine_rhs, jac0, shift0)
    mid_rhs = restrict(residual(fine, fine_rhs, jac0, shift0))
    middle = relax(mid_rhs, jac1, shift1)
    middle = sweep(middle, mid_rhs, jac1, shift1)
    coarse_rhs = restrict(residual(middle, mid_rhs, jac1, shift1))
    coarse = relax(coarse_rhs, jac2, shift2)
    for step in range(COARSE_SWEEPS - 1):
        coarse = sweep(coarse, coarse_rhs, jac2, shift2)
    middle = middle + prolong(coarse)
    middle = sweep(middle, mid_rhs, jac1, shift1)
    middle = sweep(middle, mid_rhs, jac1, shift1)
    fine = fine + prolong(middle)
    fine = sweep(fine, fine_rhs, jac0, shift0)
    fine = sweep(fine, fine_rhs, jac0, shift0)
    weights = blade_mask.astype(jnp.float32)
    work = jnp.sum(weights * (fine[4] * fine[6] - fine[9] * fine[1]))
    cells = fine.shape[1] * fine.shape[2] * fine.shape[3]
    damping = work * (25.0 / jnp.sqrt(jnp.float32(cells)))
    return (fine.reshape(rhs.shape), damping)
```

```python
import functools

import jax
import jax.numpy as jnp
from jax import lax
from jax.experimental import pallas as pl
from jax.experimental.pallas import tpu as pltpu
from jax.sharding import PartitionSpec as P

COARSE_SWEEPS = 4
MESH = pl.DeviceIdType.MESH
W = 128
F32 = jnp.float32


class Level:
    def __init__(self, rows, planes, subs, dup):
        self.nr, self.np, self.subs, self.dup = rows, planes, subs, dup
        self.sp = planes * subs
        self.pad = planes + 2
        self.npl = self.pad * subs
        self.nr8 = max(rows, 8)
        self.height = self.nr8 + 16
        self.per = 64 // (dup * self.sp)
        self.packs = -(-10 // self.per)


FINE = Level(16, 8, 1, 1)
MID = Level(8, 4, 2, 2)
COARSE = Level(4, 2, 2, 4)


def lanes(rows):
    return lax.broadcasted_iota(jnp.int32, (rows, W), 1)


def roll(x, shift):
    return pltpu.roll(x, shift, 1)


def join(a, b):
    return jnp.where((lanes(a.shape[0]) & 1) == 0, a, b)


def split(w):
    even = (lanes(w.shape[0]) & 1) == 0
    return jnp.where(even, w, roll(w, 1)), jnp.where(even, roll(w, W - 1), w)


def scratch():
    shapes = {}

    def vmem(name, *shape):
        shapes[name] = pltpu.VMEM(shape, F32)

    for tag, lv in (("0", FINE), ("1", MID), ("2", COARSE)):
        vmem("ua" + tag, 10 * lv.npl, lv.height, W)
        vmem("ub" + tag, 10 * lv.npl, lv.height, W)
        vmem("f" + tag, 10 * lv.sp, lv.nr8, W)
        vmem("c" + tag, 26 * lv.sp, lv.nr8, W)
        vmem("sr" + tag, 5 * lv.sp, lv.nr8, W)
        vmem("si" + tag, 5 * lv.sp, lv.nr8, W)
    for r in range(ROUNDS):
        lv = LEVEL_OF[r]
        tag = "_%d" % r
        fields, ends = (10, 2) if lv is FINE else (5, 4)
        vmem("axs" + tag, ends, fields, lv.nr8, W)
        vmem("axr" + tag, ends, fields, lv.nr8, W)
        vmem("rs" + tag, 2, lv.sp, 16 if lv is FINE else 8, W)
        vmem("rr" + tag, 2, lv.sp, 16 if lv is FINE else 8, W)
        vmem("ps" + tag, lv.packs, lv.nr8, W)
        vmem("pr" + tag, 2, lv.packs, lv.nr8, W)
        vmem("m" + tag, lv.packs, lv.nr8, W)
    vmem("part_s", 2, 5, 8, W)
    vmem("part_r", 2, 5, 8, W)
    vmem("f_part", 40, 8, W)
    vmem("gs", 20, 8, W)
    vmem("gr", 20, 8, W)
    vmem("c1s", 52, 8, W)
    vmem("c1r", 52, 8, W)
    vmem("c2s", 26, 8, W)
    vmem("c2r", 26, 8, W)
    vmem("t", 10, 48, W)
    vmem("j1", 104, 8, 64)
    vmem("j2", 52, 4, 32)
    vmem("j2p", 52, 8, 32)
    vmem("outv", 80, 16, W)
    vmem("red0", 16, 8, W)
    vmem("red1", 16, 8, W)
    shapes["mask"] = pltpu.VMEM((8, 16, W), jnp.int32)
    shapes["ss"] = pltpu.SemaphoreType.DMA((COPIES,))
    shapes["rs"] = pltpu.SemaphoreType.DMA((COPIES,))
    shapes["ls"] = pltpu.SemaphoreType.DMA((10,))
    return shapes


LEVEL_OF = [FINE, FINE, MID, MID, COARSE, COARSE, COARSE, MID, MID, MID, FINE]
ROUNDS = len(LEVEL_OF)
COPIES = 128


def kernel(sizes, names, *refs):
    rhs, jac0, shift0, jac1, shift1, jac2, shift2, blade = refs[:8]
    out, damp = refs[8:10]
    v = dict(zip(names, refs[10:]))
    n_ax, n_rad, n_pit, cells = sizes

    ax, rad, pit = lax.axis_index("axial"), lax.axis_index("radial"), lax.axis_index("pitch")
    core = lax.rem(ax, 2)
    zh = lax.rem(ax // 2, 2)
    x = ax // 4
    nx = n_ax // 4
    z = zh * n_pit + pit
    nz = 2 * n_pit

    def place(xx, yy, zz, cc):
        return {"axial": xx * 4 + (zz // n_pit) * 2 + cc, "radial": yy, "pitch": lax.rem(zz, n_pit)}

    up, down = {"axial": ax + 1}, {"axial": ax - 1}
    has_up, has_down = ax < n_ax - 1, ax > 0
    north, south = {"radial": rad + 1}, {"radial": rad - 1}
    has_north, has_south = rad < n_rad - 1, rad > 0
    east, west = {"pitch": lax.rem(pit + 1, n_pit)}, {"pitch": lax.rem(pit + n_pit - 1, n_pit)}
    z_east, z_west = place(x, rad, lax.rem(z + 1, nz), core), place(x, rad, lax.rem(z + nz - 1, nz), core)
    twin = {"axial": ax + 2 - 4 * zh}
    sibling = {"axial": ax + 1 - 2 * core}
    hop = {"axial": ax + 6 * core - 3}
    has_hop = jnp.logical_or(jnp.logical_and(core == 0, x > 0), jnp.logical_and(core == 1, x < nx - 1))
    wrap_e = pit == n_pit - 1
    wrap_w = pit == 0

    def when(cond, act):
        if cond is None:
            act()
        else:
            pl.when(cond)(act)

    local = [
        (rhs, v["f0"]),
        (jac0, v["c0"].at[pl.ds(0, 200)]),
        (shift0, v["c0"].at[pl.ds(200, 8)]),
        (jac1, v["j1"].at[pl.ds(0, 100)]),
        (shift1, v["j1"].at[pl.ds(100, 4)]),
        (jac2, v["j2"].at[pl.ds(0, 50)]),
        (shift2, v["j2"].at[pl.ds(50, 2)]),
        (blade, v["mask"]),
    ]
    loads = [pltpu.make_async_copy(a, b, v["ls"].at[i]) for i, (a, b) in enumerate(local)]
    for c in loads:
        c.start()

    barrier = pltpu.get_barrier_semaphore()
    greet = [
        (up, has_up),
        (down, has_down),
        (north, has_north),
        (south, has_south),
        (east, None),
        (west, None),
        (twin, None),
        (hop, has_hop),
        (z_east, wrap_e),
        (z_west, wrap_w),
    ]
    for dev, cond in greet:
        when(cond, lambda dev=dev: pl.semaphore_signal(barrier, inc=1, device_id=dev, device_id_type=MESH))

    counter = [0]
    sent = []

    class Msg:
        def __init__(self, src, dst, dev, send_if=None, recv_if=None, landing=None):
            i = counter[0]
            counter[0] += 1
            make = lambda d: pltpu.make_async_remote_copy(
                src_ref=src, dst_ref=d, send_sem=v["ss"].at[i], recv_sem=v["rs"].at[i], device_id=dev, device_id_type=MESH
            )
            self.copy = make(dst)
            self.into = self.copy if landing is None else make(landing)
            self.send_if, self.recv_if = send_if, recv_if

        def start(self):
            when(self.send_if, self.copy.start)
            sent.append(self)

        def recv(self):
            when(self.recv_if, self.into.wait_recv)

    for r in range(ROUNDS):
        tag = "_%d" % r
        axr, rr = v["axr" + tag], v["rr" + tag]

        def zero(ref, i):
            ref[i] = jnp.zeros(ref.shape[1:], F32)

        if LEVEL_OF[r] is FINE:
            when(jnp.logical_not(has_down), functools.partial(zero, axr, 0))
            when(jnp.logical_not(has_up), functools.partial(zero, axr, 1))
        else:
            when(jnp.logical_and(core == 0, x == 0), functools.partial(zero, axr, 0))
            when(jnp.logical_and(core == 1, x == nx - 1), functools.partial(zero, axr, 3))
        when(jnp.logical_not(has_south), functools.partial(zero, rr, 0))
        when(jnp.logical_not(has_north), functools.partial(zero, rr, 1))
    part_s, part_r = v["part_s"], v["part_r"]
    when(jnp.logical_not(has_down), lambda: zero(part_r, 0))
    when(jnp.logical_not(has_up), lambda: zero(part_r, 1))

    def planes(lv, body, lo=0, hi=None, step=1):
        hi = lv.np if hi is None else hi
        for s in range(lv.subs):

            def go(a, carry, s=s):
                a = lo + a * step
                body(s * lv.np + a, s * lv.pad + 1 + a)
                return carry

            lax.fori_loop(0, (hi - lo + step - 1) // step, go, 0)

    def coefficients(lv, tag):
        c, sr, si = v["c" + tag], v["sr" + tag], v["si" + tag]

        def body(sp, carry):
            s = c[25 * lv.sp + sp, 0 : lv.nr, :]
            for i in range(5):
                d = c[6 * i * lv.sp + sp, 0 : lv.nr, :]
                denom = d * d + s * s
                inv = 0.7 / jnp.where(denom > 0, denom, 1.0)
                sr[i * lv.sp + sp, 0 : lv.nr, :] = d * inv
                si[i * lv.sp + sp, 0 : lv.nr, :] = s * inv
            return carry

        lax.fori_loop(0, lv.sp, body, 0)

    def smooth(lv, tag, sp, res):
        sr, si = v["sr" + tag], v["si" + tag]
        new = [None] * 10
        for i in range(5):
            a, b = sr[i * lv.sp + sp, 0 : lv.nr, :], si[i * lv.sp + sp, 0 : lv.nr, :]
            new[i] = a * res[i] + b * res[5 + i]
            new[5 + i] = a * res[5 + i] - b * res[i]
        return new

    def first(lv, tag, u):
        f = v["f" + tag]

        def body(sp, pp):
            new = smooth(lv, tag, sp, [f[k * lv.sp + sp, 0 : lv.nr, :] for k in range(10)])
            for k in range(10):
                u[k * lv.npl + pp, 8 : 8 + lv.nr, :] = new[k]

        planes(lv, body)

    def pack_inplane(lv, u, r):
        tag = "_%d" % r
        rs, ps = v["rs" + tag], v["ps" + tag]
        d, nr = lv.dup, lv.nr
        group = lanes(nr) // (2 * d)
        carry = tuple(jnp.zeros((nr, W), F32) for _ in range(lv.packs))
        for s in range(lv.subs):

            def body(a, carry, s=s):
                sp, pp = s * lv.np + a, s * lv.pad + 1 + a
                packed = list(carry)
                xs = [u[k * lv.npl + pp, 8 : 8 + nr, :] for k in range(10)]
                for k in range(10):
                    slot, j = (k % lv.per) * lv.sp + sp, k // lv.per
                    packed[j] = jnp.where(group == slot, roll(xs[k], d + 2 * d * slot), packed[j])
                faces = xs if lv is FINE else [join(xs[k], xs[5 + k]) for k in range(5)]
                for k, w in enumerate(faces):
                    rs[0, sp, k : k + 1, :] = w[0:1, :]
                    rs[1, sp, k : k + 1, :] = w[nr - 1 : nr, :]
                return tuple(packed)

            carry = lax.fori_loop(0, lv.np, body, carry)
        for j in range(lv.packs):
            ps[j, 0:nr, :] = carry[j]

    def inplane_msgs(lv, r):
        tag = "_%d" % r
        rs, rr, ps, pr = (v[n + tag] for n in ("rs", "rr", "ps", "pr"))
        e, w = (east, west) if lv is FINE else (z_east, z_west)
        return [
            Msg(ps, pr.at[0], e),
            Msg(ps, pr.at[1], w),
            Msg(rs.at[1], rr.at[0], north, has_north, has_south),
            Msg(rs.at[0], rr.at[1], south, has_south, has_north),
        ]

    def pack_axial(lv, u, r):
        axs = v["axs_%d" % r]
        nr = lv.nr
        if lv is FINE:

            def body(k, carry):
                axs[0, k] = u[k * lv.npl + 1, 8 : 8 + nr, :]
                axs[1, k] = u[k * lv.npl + lv.np, 8 : 8 + nr, :]
                return carry

            lax.fori_loop(0, 10, body, 0)
            return
        for q in range(4):
            pp = (q // 2) * lv.pad + (1 if q % 2 == 0 else lv.np)
            for k in range(5):
                axs[q, k, 0:nr, :] = join(
                    u[k * lv.npl + pp, 8 : 8 + nr, :], u[(5 + k) * lv.npl + pp, 8 : 8 + nr, :]
                )

    def axial_msgs(lv, r):
        axs, axr = v["axs_%d" % r], v["axr_%d" % r]
        if lv is FINE:
            return [
                Msg(axs.at[1], axr.at[0], up, has_up, has_down),
                Msg(axs.at[0], axr.at[1], down, has_down, has_up),
            ]
        return [
            Msg(axs.at[3 * core], axr.at[3 - 3 * core], hop, has_hop, has_hop, landing=axr.at[3 * core]),
            Msg(axs.at[pl.ds(1 - core, 3)], axr.at[pl.ds(core, 3)], sibling, landing=axr.at[pl.ds(1 - core, 3)]),
        ]

    def land_axial(lv, u, r):
        axr = v["axr_%d" % r]
        nr = lv.nr
        if lv is FINE:

            def body(k, carry):
                u[k * lv.npl, 8 : 8 + nr, :] = axr[0, k]
                u[k * lv.npl + lv.np + 1, 8 : 8 + nr, :] = axr[1, k]
                return carry

            lax.fori_loop(0, 10, body, 0)
            return
        for q in range(4):
            pp = (q // 2) * lv.pad + (0 if q % 2 == 0 else lv.np + 1)
            for k in range(5):
                re, im = split(axr[q, k, 0:nr, :])
                u[k * lv.npl + pp, 8 : 8 + nr, :] = re
                u[(5 + k) * lv.npl + pp, 8 : 8 + nr, :] = im

    def land_inplane(lv, u, r):
        tag = "_%d" % r
        rr, pr, m = (v[n + tag] for n in ("rr", "pr", "m"))
        d, nr = lv.dup, lv.nr
        low = (lanes(nr) & (2 * d - 1)) < d
        for j in range(lv.packs):
            m[j, 0:nr, :] = jnp.where(low, roll(pr[1, j, 0:nr, :], W - d), roll(pr[0, j, 0:nr, :], d))

        def body(sp, pp):
            for side, row in ((0, 7), (1, 8 + nr)):
                if lv is FINE:
                    for k in range(10):
                        u[k * lv.npl + pp, row : row + 1, :] = rr[side, sp, k : k + 1, :]
                else:
                    re, im = split(rr[side, sp])
                    for k in range(5):
                        u[k * lv.npl + pp, row : row + 1, :] = re[k : k + 1, :]
                        u[(5 + k) * lv.npl + pp, row : row + 1, :] = im[k : k + 1, :]

        planes(lv, body)

    def side_halo(lv, r):
        m = v["m_%d" % r]
        d = lv.dup
        return lambda k, sp: roll(m[k // lv.per, 0 : lv.nr, :], W - d - 2 * d * ((k % lv.per) * lv.sp + sp))

    def residual(lv, tag, u, sp, pp, halo):
        f, c = v["f" + tag], v["c" + tag]
        d, nr = lv.dup, lv.nr
        lane = lanes(nr)
        first_lane, last_lane = lane < d, lane >= W - d
        xs, res = [], []
        for k in range(10):
            b = k * lv.npl + pp
            c0 = u[b, 8 : 8 + nr, :]
            y = f[k * lv.sp + sp, 0:nr, :] + (u[b + 1, 8 : 8 + nr, :] + u[b - 1, 8 : 8 + nr, :])
            y = y + (u[b, 7 : 7 + nr, :] + u[b, 9 : 9 + nr, :])
            h = halo(k, sp)
            y = y + (jnp.where(first_lane, h, roll(c0, d)) + jnp.where(last_lane, h, roll(c0, W - d)))
            xs.append(c0)
            res.append(y)
        s = c[25 * lv.sp + sp, 0:nr, :]
        for i in range(5):
            re, im = res[i] + s * xs[5 + i], res[5 + i] - s * xs[i]
            for j in range(5):
                a = c[(5 * i + j) * lv.sp + sp, 0:nr, :]
                re = re - a * xs[j]
                im = im - a * xs[5 + j]
            res[i], res[5 + i] = re, im
        return xs, res

    def sweep(lv, tag, u, new, halo):
        def body(sp, pp):
            xs, res = residual(lv, tag, u, sp, pp, halo)
            corr = smooth(lv, tag, sp, res)
            for k in range(10):
                new[k * lv.npl + pp, 8 : 8 + lv.nr, :] = xs[k] + corr[k]

        return body

    t = v["t"]

    def fold(lv, k, y):
        d, nr = lv.dup, lv.nr
        y = y + jnp.where((lanes(nr) & d) == 0, roll(y, W - d), roll(y, d))
        t[k, 0:nr, :] = y
        return t[k, pl.ds(0, nr // 2, stride=2), :] + t[k, pl.ds(1, nr // 2, stride=2), :]

    def exchange(lv, u, r):
        pack_axial(lv, u, r)
        a = axial_msgs(lv, r)
        for msg in a:
            msg.start()
        pack_inplane(lv, u, r)
        b = inplane_msgs(lv, r)
        for msg in b:
            msg.start()
        for msg in b:
            msg.recv()
        land_inplane(lv, u, r)
        for msg in a:
            msg.recv()
        land_axial(lv, u, r)

    ua, ub = v["ua0"], v["ub0"]
    f1, c1, c2 = v["f1"], v["c1"], v["c2"]

    for c in loads[:3]:
        c.wait()
    coefficients(FINE, "0")
    first(FINE, "0", ua)

    pack_axial(FINE, ua, 0)
    count = sum(jnp.int32(1) if cond is None else cond.astype(jnp.int32) for _, cond in greet)
    pl.semaphore_wait(barrier, count)
    a0 = axial_msgs(FINE, 0)
    for msg in a0:
        msg.start()
    pack_inplane(FINE, ua, 0)
    b0 = inplane_msgs(FINE, 0)
    for msg in b0:
        msg.start()

    for c in loads[3:]:
        c.wait()

    def spreader(n):
        return (
            lax.broadcasted_iota(jnp.int32, (n, W), 1) // (W // n) == lax.broadcasted_iota(jnp.int32, (n, W), 0)
        ).astype(F32)

    def spread(cells_in, n):
        rows = cells_in.shape[0] * 8
        y = jnp.dot(
            cells_in.reshape(rows, n), spreader(n), precision=lax.Precision.HIGHEST, preferred_element_type=F32
        )
        return y.reshape(cells_in.shape[0], 8, W)

    j1, j2, j2p = v["j1"], v["j2"], v["j2p"]
    c1s, c1r, c2s, c2r = v["c1s"], v["c1r"], v["c2s"], v["c2r"]

    def spread1(e, carry):
        c1[pl.ds(e * 8 + zh * 4, 4)] = spread(j1[pl.ds(e * 4, 4)], 64)
        return carry

    lax.fori_loop(0, 26, spread1, 0)

    def place2(i, carry):
        j2p[i, 0:4, :] = j2[i]
        j2p[i, 4:8, :] = j2[i]
        return carry

    lax.fori_loop(0, 52, place2, 0)

    def spread2(e, carry):
        y = spread(j2p[pl.ds(e * 4, 4)], 32)
        c2[pl.ds(e * 8 + zh * 2, 2)] = y[0:2]
        c2[pl.ds(e * 8 + 4 + zh * 2, 2)] = y[2:4]
        return carry

    lax.fori_loop(0, 13, spread2, 0)

    def join1(e, carry):
        for a in range(4):
            c1s[e * 4 + a] = join(c1[e * 8 + zh * 4 + a], c1[(e + 13) * 8 + zh * 4 + a])
        for a in range(2):
            c2s[e * 2 + a] = join(c2[e * 4 + zh * 2 + a], c2[(e + 13) * 4 + zh * 2 + a])
        return carry

    lax.fori_loop(0, 13, join1, 0)

    def clear(k, carry):
        ub[k * FINE.npl] = jnp.zeros((32, W), F32)
        ub[k * FINE.npl + FINE.np + 1] = jnp.zeros((32, W), F32)
        return carry

    lax.fori_loop(0, 10, clear, 0)

    for msg in b0:
        msg.recv()
    land_inplane(FINE, ua, 0)
    body = sweep(FINE, "0", ua, ub, side_halo(FINE, 0))
    planes(FINE, body, 1, 7)
    for msg in a0:
        msg.recv()
    land_axial(FINE, ua, 0)
    planes(FINE, body, 0, 8, 7)

    for end in range(2):
        for k in range(5):
            pp = 1 if end == 0 else FINE.np
            part_s[end, k] = join(
                fold(FINE, k, ub[k * FINE.npl + pp, 8:24, :]),
                fold(FINE, 5 + k, ub[(5 + k) * FINE.npl + pp, 8:24, :]),
            )
    parts = [
        Msg(part_s.at[1], part_r.at[0], up, has_up, has_down),
        Msg(part_s.at[0], part_r.at[1], down, has_down, has_up),
    ]
    for msg in parts:
        msg.start()
    pack_inplane(FINE, ub, 1)
    b1 = inplane_msgs(FINE, 1)
    for msg in b1:
        msg.start()
    mc1 = Msg(c1s, c1r, twin)
    mc2 = Msg(c2s, c2r, twin)
    mc1.start()
    mc2.start()
    for msg in b1:
        msg.recv()
    land_inplane(FINE, ub, 1)
    f_part = v["f_part"]
    halo1 = side_halo(FINE, 1)

    def restrict0(a, carry):
        _, r0 = residual(FINE, "0", ub, 2 * a, 2 * a + 1, halo1)
        _, r1 = residual(FINE, "0", ub, 2 * a + 1, 2 * a + 2, halo1)
        for k in range(10):
            f_part[k * 4 + a] = 0.125 * fold(FINE, k, r0[k] + r1[k])
        return carry

    lax.fori_loop(0, 4, restrict0, 0)
    for msg in parts:
        msg.recv()
    gs, gr = v["gs"], v["gr"]
    for k in range(5):
        for end, a in ((0, 0), (1, 3)):
            re, im = split(part_r[end, k])
            f_part[k * 4 + a] = f_part[k * 4 + a] + 0.125 * re
            f_part[(5 + k) * 4 + a] = f_part[(5 + k) * 4 + a] + 0.125 * im

    def gather(i, carry):
        gs[i] = join(f_part[i], f_part[20 + i])
        return carry

    lax.fori_loop(0, 20, gather, 0)
    mg = Msg(gs, gr, twin)
    mg.start()
    pack_axial(FINE, ub, 1)
    a1 = axial_msgs(FINE, 1)
    for msg in a1:
        msg.start()
    for k in range(10):
        f1[pl.ds(k * 8 + zh * 4, 4)] = f_part[k * 4 : k * 4 + 4]
    mc1.recv()
    mc2.recv()

    def split1(e, carry):
        for a in range(4):
            lo, hi = split(c1r[e * 4 + a])
            c1[e * 8 + (1 - zh) * 4 + a] = lo
            c1[(e + 13) * 8 + (1 - zh) * 4 + a] = hi
        for a in range(2):
            lo, hi = split(c2r[e * 2 + a])
            c2[e * 4 + (1 - zh) * 2 + a] = lo
            c2[(e + 13) * 4 + (1 - zh) * 2 + a] = hi
        return carry

    lax.fori_loop(0, 13, split1, 0)
    coefficients(MID, "1")
    coefficients(COARSE, "2")
    mg.recv()

    def land_gather(i, carry):
        re, im = split(gr[i])
        k, a = i // 4, lax.rem(i, 4)
        f1[k * 8 + (1 - zh) * 4 + a] = re
        f1[(k + 5) * 8 + (1 - zh) * 4 + a] = im
        return carry

    lax.fori_loop(0, 20, land_gather, 0)

    m_a, m_b = v["ua1"], v["ub1"]
    first(MID, "1", m_a)
    exchange(MID, m_a, 2)
    planes(MID, sweep(MID, "1", m_a, m_b, side_halo(MID, 2)))
    exchange(MID, m_b, 3)
    halo3 = side_halo(MID, 3)
    f2 = v["f2"]
    for s in range(2):

        def restrict1(a, carry, s=s):
            _, r0 = residual(MID, "1", m_b, s * 4 + 2 * a, s * 6 + 2 * a + 1, halo3)
            _, r1 = residual(MID, "1", m_b, s * 4 + 2 * a + 1, s * 6 + 2 * a + 2, halo3)
            for k in range(10):
                f2[k * 4 + s * 2 + a, 0:4, :] = 0.125 * fold(MID, k, r0[k] + r1[k])
            return carry

        lax.fori_loop(0, 2, restrict1, 0)

    q_a, q_b = v["ua2"], v["ub2"]
    first(COARSE, "2", q_a)
    for step in range(COARSE_SWEEPS - 1):
        exchange(COARSE, q_a, 4 + step)
        planes(COARSE, sweep(COARSE, "2", q_a, q_b, side_halo(COARSE, 4 + step)))
        q_a, q_b = q_b, q_a

    for s in range(2):

        def prolong1(a, carry, s=s):
            for k in range(10):
                w = q_a[k * COARSE.npl + s * 4 + 1 + a // 2, 8:16, :]
                t[k, pl.ds(0, 8, stride=2), :] = w
                t[k, pl.ds(1, 8, stride=2), :] = w
                b = k * MID.npl + s * 6 + 1 + a
                m_b[b, 8:16, :] = m_b[b, 8:16, :] + t[k, 0:8, :]
            return carry

        lax.fori_loop(0, 4, prolong1, 0)
    exchange(MID, m_b, 7)
    planes(MID, sweep(MID, "1", m_b, m_a, side_halo(MID, 7)))
    exchange(MID, m_a, 8)
    planes(MID, sweep(MID, "1", m_a, m_b, side_halo(MID, 8)))

    for msg in a1:
        msg.recv()
    land_axial(FINE, ub, 1)
    exchange(MID, m_b, 9)

    def prolong0(q, carry):
        for k in range(10):
            w = m_b[k * MID.npl + zh * 6 + (q + 1) // 2]
            t[k, pl.ds(0, 24, stride=2), :] = w
            t[k, pl.ds(1, 24, stride=2), :] = w
            ub[k * FINE.npl + q] = ub[k * FINE.npl + q] + t[k, 8:40, :]
        return carry

    lax.fori_loop(0, 10, prolong0, 0)
    halo9 = side_halo(MID, 9)

    def halo_up(k, sp):
        w = halo9(k, zh * 4 + sp // 2)
        t[k, pl.ds(0, 8, stride=2), :] = w
        t[k, pl.ds(1, 8, stride=2), :] = w
        return halo1(k, sp) + t[k, 0:16, :]

    planes(FINE, sweep(FINE, "0", ub, ua, halo_up))

    pack_axial(FINE, ua, 10)
    a10 = axial_msgs(FINE, 10)
    for msg in a10:
        msg.start()
    pack_inplane(FINE, ua, 10)
    b10 = inplane_msgs(FINE, 10)
    for msg in b10:
        msg.start()
    for msg in b10:
        msg.recv()
    land_inplane(FINE, ua, 10)
    outv, mask = v["outv"], v["mask"]
    halo10 = side_halo(FINE, 10)

    def last(a, acc):
        xs, res = residual(FINE, "0", ua, a, a + 1, halo10)
        corr = smooth(FINE, "0", a, res)
        new = [xs[k] + corr[k] for k in range(10)]
        for k in range(10):
            outv[k * 8 + a] = new[k]
        return acc + mask[a].astype(F32) * (new[4] * new[6] - new[9] * new[1])

    acc = lax.fori_loop(1, 7, last, jnp.zeros((16, W), F32))
    for msg in a10:
        msg.recv()
    land_axial(FINE, ua, 10)
    acc = lax.fori_loop(0, 2, lambda i, c: last(7 * i, c), acc)
    store = pltpu.make_async_copy(outv, out, v["ls"].at[8])
    store.start()

    red0, red1 = v["red0"], v["red1"]
    mine0 = x * n_rad + rad
    red0[mine0] = acc[0:8] + acc[8:16]
    msgs = []
    n0 = nx * n_rad
    for off in range(1, n0):
        to = lax.rem(mine0 + off, n0)
        back = lax.rem(mine0 + n0 - off, n0)
        msgs.append(
            Msg(red0.at[mine0], red0.at[mine0], place(to // n_rad, lax.rem(to, n_rad), z, core), landing=red0.at[back])
        )
    for msg in msgs:
        msg.start()
    for msg in msgs:
        msg.recv()
    total = red0[0]
    for i in range(1, n0):
        total = total + red0[i]
    mine1 = z * 2 + core
    red1[mine1] = total
    msgs = []
    n1 = nz * 2
    for off in range(1, n1):
        to = lax.rem(mine1 + off, n1)
        back = lax.rem(mine1 + n1 - off, n1)
        msgs.append(Msg(red1.at[mine1], red1.at[mine1], place(x, rad, to // 2, lax.rem(to, 2)), landing=red1.at[back]))
    for msg in msgs:
        msg.start()
    for msg in msgs:
        msg.recv()
    total = red1[0]
    for i in range(1, n1):
        total = total + red1[i]
    damp[0, 0] = jnp.sum(total) * (25.0 / jnp.sqrt(jnp.float32(cells)))
    store.wait()
    for msg in sent:
        when(msg.send_if, msg.copy.wait_send)


def solution(mesh):
    sizes = (mesh.shape["axial"], mesh.shape["radial"], mesh.shape["pitch"])

    def on_device(rhs, jac0, shift0, jac1, shift1, jac2, shift2, blade_mask):
        cells = shift0.size * sizes[0] * sizes[1] * sizes[2]
        shapes = scratch()
        out, damp = pl.pallas_call(
            functools.partial(kernel, sizes + (cells,), tuple(shapes)),
            out_shape=(jax.ShapeDtypeStruct((80, 16, W), F32), jax.ShapeDtypeStruct((1, 1), F32)),
            in_specs=[pl.BlockSpec(memory_space=pl.ANY)] * 8,
            out_specs=(pl.BlockSpec(memory_space=pl.ANY), pl.BlockSpec(memory_space=pltpu.SMEM)),
            scratch_shapes=list(shapes.values()),
            compiler_params=pltpu.CompilerParams(
                collective_id=0, has_side_effects=True, vmem_limit_bytes=48 * 1024 * 1024
            ),
        )(
            rhs.reshape(80, 16, W),
            jac0.reshape(200, 16, W),
            shift0,
            jac1.reshape(100, 8, 64),
            shift1,
            jac2.reshape(50, 4, 32),
            shift2,
            blade_mask,
        )
        return out.reshape(rhs.shape), damp.reshape(())

    spec = P(None, None, "axial", "radial", "pitch")
    flat = P("axial", "radial", "pitch")
    return jax.shard_map(
        on_device,
        mesh=mesh,
        in_specs=(spec, spec, flat, spec, flat, spec, flat, flat),
        out_specs=(spec, P()),
        check_vma=False,
    )
```

```python
import functools

import jax
import jax.numpy as jnp
from jax import lax
from jax.experimental import pallas as pl
from jax.experimental.pallas import tpu as pltpu
from jax.sharding import PartitionSpec as P

COARSE_SWEEPS = 4
MESH = pl.DeviceIdType.MESH
W = 128
F32 = jnp.float32


class Level:
    def __init__(self, rows, planes, subs, dup):
        self.nr, self.np, self.subs, self.dup = rows, planes, subs, dup
        self.sp = planes * subs
        self.pad = planes + 2
        self.npl = self.pad * subs
        self.nr8 = max(rows, 8)
        self.height = self.nr8 + 16
        self.per = 64 // (dup * self.sp)
        self.packs = -(-10 // self.per)


FINE = Level(16, 8, 1, 1)
MID = Level(8, 4, 2, 2)
COARSE = Level(4, 2, 2, 4)


def lanes(rows):
    return lax.broadcasted_iota(jnp.int32, (rows, W), 1)


def roll(x, shift):
    return pltpu.roll(x, shift, 1)


def join(a, b):
    return jnp.where((lanes(a.shape[0]) & 1) == 0, a, b)


def split(w):
    even = (lanes(w.shape[0]) & 1) == 0
    return jnp.where(even, w, roll(w, 1)), jnp.where(even, roll(w, W - 1), w)


def scratch():
    shapes = {}

    def vmem(name, *shape):
        shapes[name] = pltpu.VMEM(shape, F32)

    for tag, lv in (("0", FINE), ("1", MID), ("2", COARSE)):
        vmem("ua" + tag, 10 * lv.npl, lv.height, W)
        vmem("ub" + tag, 10 * lv.npl, lv.height, W)
        vmem("f" + tag, 10 * lv.sp, lv.nr8, W)
        vmem("c" + tag, 26 * lv.sp, lv.nr8, W)
        vmem("sr" + tag, 5 * lv.sp, lv.nr8, W)
        vmem("si" + tag, 5 * lv.sp, lv.nr8, W)
    for r in range(ROUNDS):
        lv = LEVEL_OF[r]
        tag = "_%d" % r
        fields, ends = (10, 2) if lv is FINE else (5, 4)
        vmem("axs" + tag, ends, fields, lv.nr8, W)
        vmem("axr" + tag, ends, fields, lv.nr8, W)
        vmem("rs" + tag, 2, lv.sp, 16 if lv is FINE else 8, W)
        vmem("rr" + tag, 2, lv.sp, 16 if lv is FINE else 8, W)
        vmem("ps" + tag, lv.packs, lv.nr8, W)
        vmem("pr" + tag, 2, lv.packs, lv.nr8, W)
        vmem("m" + tag, lv.packs, lv.nr8, W)
    vmem("part_s", 2, 5, 8, W)
    vmem("part_r", 2, 5, 8, W)
    vmem("f_part", 40, 8, W)
    vmem("gs", 20, 8, W)
    vmem("gr", 20, 8, W)
    vmem("c1s", 52, 8, W)
    vmem("c1r", 52, 8, W)
    vmem("c2s", 13, 8, W)
    vmem("c2r", 13, 8, W)
    vmem("t", 10, 48, W)
    vmem("j1", 104, 8, 64)
    vmem("j2", 52, 4, 32)
    vmem("j2p", 26, 8, 32)
    vmem("red0", 16, 8, W)
    vmem("red1", 16, 8, W)
    shapes["mask"] = pltpu.VMEM((8, 16, W), jnp.int32)
    shapes["ss"] = pltpu.SemaphoreType.DMA((COPIES,))
    shapes["rs"] = pltpu.SemaphoreType.DMA((COPIES,))
    shapes["ls"] = pltpu.SemaphoreType.DMA((10,))
    return shapes


LEVEL_OF = [FINE, FINE, MID, MID, COARSE, COARSE, COARSE, MID, MID, MID, FINE]
ROUNDS = len(LEVEL_OF)
COPIES = 128
UNROLL = 2


def kernel(sizes, names, *refs):
    rhs, jac0, shift0, jac1, shift1, jac2, shift2, blade = refs[:8]
    out, damp = refs[8:10]
    v = dict(zip(names, refs[10:]))
    n_ax, n_rad, n_pit, cells = sizes

    ax, rad, pit = lax.axis_index("axial"), lax.axis_index("radial"), lax.axis_index("pitch")
    core = lax.rem(ax, 2)
    zh = lax.rem(ax // 2, 2)
    x = ax // 4
    nx = n_ax // 4
    z = zh * n_pit + pit
    nz = 2 * n_pit

    def place(xx, yy, zz, cc):
        return {"axial": xx * 4 + (zz // n_pit) * 2 + cc, "radial": yy, "pitch": lax.rem(zz, n_pit)}

    up, down = {"axial": ax + 1}, {"axial": ax - 1}
    has_up, has_down = ax < n_ax - 1, ax > 0
    north, south = {"radial": rad + 1}, {"radial": rad - 1}
    has_north, has_south = rad < n_rad - 1, rad > 0
    east, west = {"pitch": lax.rem(pit + 1, n_pit)}, {"pitch": lax.rem(pit + n_pit - 1, n_pit)}
    z_east, z_west = place(x, rad, lax.rem(z + 1, nz), core), place(x, rad, lax.rem(z + nz - 1, nz), core)
    twin = {"axial": ax + 2 - 4 * zh}
    sibling = {"axial": ax + 1 - 2 * core}
    hop = {"axial": ax + 6 * core - 3}
    has_hop = jnp.logical_or(jnp.logical_and(core == 0, x > 0), jnp.logical_and(core == 1, x < nx - 1))
    wrap_e = pit == n_pit - 1
    wrap_w = pit == 0

    def when(cond, act):
        if cond is None:
            act()
        else:
            pl.when(cond)(act)

    local = [
        (rhs, v["f0"]),
        (jac0, v["c0"].at[pl.ds(0, 200)]),
        (shift0, v["c0"].at[pl.ds(200, 8)]),
        (jac1, v["j1"].at[pl.ds(0, 100)]),
        (shift1, v["j1"].at[pl.ds(100, 4)]),
        (jac2, v["j2"].at[pl.ds(0, 50)]),
        (shift2, v["j2"].at[pl.ds(50, 2)]),
        (blade, v["mask"]),
    ]
    loads = [pltpu.make_async_copy(a, b, v["ls"].at[i]) for i, (a, b) in enumerate(local)]
    for c in loads:
        c.start()

    barrier = pltpu.get_barrier_semaphore()
    greet = [
        (up, has_up),
        (down, has_down),
        (north, has_north),
        (south, has_south),
        (east, None),
        (west, None),
        (twin, None),
        (hop, has_hop),
        (z_east, wrap_e),
        (z_west, wrap_w),
    ]
    for dev, cond in greet:
        when(cond, lambda dev=dev: pl.semaphore_signal(barrier, inc=1, device_id=dev, device_id_type=MESH))

    counter = [0]
    sent = []

    class Msg:
        def __init__(self, src, dst, dev, send_if=None, recv_if=None, landing=None):
            i = counter[0]
            counter[0] += 1
            make = lambda d: pltpu.make_async_remote_copy(
                src_ref=src, dst_ref=d, send_sem=v["ss"].at[i], recv_sem=v["rs"].at[i], device_id=dev, device_id_type=MESH
            )
            self.copy = make(dst)
            self.into = self.copy if landing is None else make(landing)
            self.send_if, self.recv_if = send_if, recv_if

        def start(self):
            when(self.send_if, self.copy.start)
            sent.append(self)

        def recv(self):
            when(self.recv_if, self.into.wait_recv)

    for r in range(ROUNDS):
        tag = "_%d" % r
        axr, rr = v["axr" + tag], v["rr" + tag]

        def zero(ref, i):
            ref[i] = jnp.zeros(ref.shape[1:], F32)

        if LEVEL_OF[r] is FINE:
            when(jnp.logical_not(has_down), functools.partial(zero, axr, 0))
            when(jnp.logical_not(has_up), functools.partial(zero, axr, 1))
        else:
            when(jnp.logical_and(core == 0, x == 0), functools.partial(zero, axr, 0))
            when(jnp.logical_and(core == 1, x == nx - 1), functools.partial(zero, axr, 3))
        when(jnp.logical_not(has_south), functools.partial(zero, rr, 0))
        when(jnp.logical_not(has_north), functools.partial(zero, rr, 1))
    part_s, part_r = v["part_s"], v["part_r"]
    when(jnp.logical_not(has_down), lambda: zero(part_r, 0))
    when(jnp.logical_not(has_up), lambda: zero(part_r, 1))

    def planes(lv, body, lo=0, hi=None, step=1):
        hi = lv.np if hi is None else hi
        for s in range(lv.subs):

            def go(a, carry, s=s):
                a = lo + a * step
                body(s * lv.np + a, s * lv.pad + 1 + a)
                return carry

            lax.fori_loop(0, (hi - lo + step - 1) // step, go, 0)

    def coefficients(lv, tag):
        c, sr, si = v["c" + tag], v["sr" + tag], v["si" + tag]

        def body(sp, carry):
            s = c[25 * lv.sp + sp, 0 : lv.nr, :]
            for i in range(5):
                d = c[6 * i * lv.sp + sp, 0 : lv.nr, :]
                denom = d * d + s * s
                inv = 0.7 / jnp.where(denom > 0, denom, 1.0)
                sr[i * lv.sp + sp, 0 : lv.nr, :] = d * inv
                si[i * lv.sp + sp, 0 : lv.nr, :] = s * inv
            return carry

        lax.fori_loop(0, lv.sp, body, 0)

    def smooth(lv, tag, sp, res):
        sr, si = v["sr" + tag], v["si" + tag]
        new = [None] * 10
        for i in range(5):
            a, b = sr[i * lv.sp + sp, 0 : lv.nr, :], si[i * lv.sp + sp, 0 : lv.nr, :]
            new[i] = a * res[i] + b * res[5 + i]
            new[5 + i] = a * res[5 + i] - b * res[i]
        return new

    def first(lv, tag, u):
        step = first_plane(lv, tag, u)
        planes(lv, lambda sp, pp: step(sp, pp) and None)

    def first_plane(lv, tag, u):
        f = v["f" + tag]

        def step(sp, pp):
            new = smooth(lv, tag, sp, [f[k * lv.sp + sp, 0 : lv.nr, :] for k in range(10)])
            for k in range(10):
                u[k * lv.npl + pp, 8 : 8 + lv.nr, :] = new[k]
            return new

        return step

    def packing(lv):
        return tuple(jnp.zeros((lv.nr, W), F32) for _ in range(lv.packs))

    def pack_plane(lv, xs, sp, r, carry):
        rs = v["rs_%d" % r]
        d, nr = lv.dup, lv.nr
        group = lanes(nr) // (2 * d)
        packed = list(carry)
        for k in range(10):
            slot, j = (k % lv.per) * lv.sp + sp, k // lv.per
            packed[j] = jnp.where(group == slot, roll(xs[k], d + 2 * d * slot), packed[j])
        faces = xs if lv is FINE else [join(xs[k], xs[5 + k]) for k in range(5)]
        for k, w in enumerate(faces):
            rs[0, sp, k : k + 1, :] = w[0:1, :]
            rs[1, sp, k : k + 1, :] = w[nr - 1 : nr, :]
        return tuple(packed)

    def pack_inplane(lv, u, r, step=None):
        ps = v["ps_%d" % r]
        carry = packing(lv)
        for s in range(lv.subs):

            def body(a, carry, s=s):
                sp, pp = s * lv.np + a, s * lv.pad + 1 + a
                if step is None:
                    xs = [u[k * lv.npl + pp, 8 : 8 + lv.nr, :] for k in range(10)]
                else:
                    xs = step(sp, pp)
                return pack_plane(lv, xs, sp, r, carry)

            carry = lax.fori_loop(0, lv.np, body, carry, unroll=UNROLL if lv is not FINE else 2)
        for j in range(lv.packs):
            ps[j, 0 : lv.nr, :] = carry[j]

    def inplane_msgs(lv, r):
        tag = "_%d" % r
        rs, rr, ps, pr = (v[n + tag] for n in ("rs", "rr", "ps", "pr"))
        e, w = (east, west) if lv is FINE else (z_east, z_west)
        return [
            Msg(ps, pr.at[0], e),
            Msg(ps, pr.at[1], w),
            Msg(rs.at[1], rr.at[0], north, has_north, has_south),
            Msg(rs.at[0], rr.at[1], south, has_south, has_north),
        ]

    def pack_axial(lv, u, r):
        axs = v["axs_%d" % r]
        nr = lv.nr
        if lv is FINE:

            def body(k, carry):
                axs[0, k] = u[k * lv.npl + 1, 8 : 8 + nr, :]
                axs[1, k] = u[k * lv.npl + lv.np, 8 : 8 + nr, :]
                return carry

            lax.fori_loop(0, 10, body, 0)
            return
        for q in range(4):
            pp = (q // 2) * lv.pad + (1 if q % 2 == 0 else lv.np)
            for k in range(5):
                axs[q, k, 0:nr, :] = join(
                    u[k * lv.npl + pp, 8 : 8 + nr, :], u[(5 + k) * lv.npl + pp, 8 : 8 + nr, :]
                )

    def axial_msgs(lv, r):
        axs, axr = v["axs_%d" % r], v["axr_%d" % r]
        if lv is FINE:
            return [
                Msg(axs.at[1], axr.at[0], up, has_up, has_down),
                Msg(axs.at[0], axr.at[1], down, has_down, has_up),
            ]
        return [
            Msg(axs.at[3 * core], axr.at[3 - 3 * core], hop, has_hop, has_hop, landing=axr.at[3 * core]),
            Msg(axs.at[pl.ds(1 - core, 3)], axr.at[pl.ds(core, 3)], sibling, landing=axr.at[pl.ds(1 - core, 3)]),
        ]

    def turn(lv, r):
        pr, m = v["pr_%d" % r], v["m_%d" % r]
        d, nr = lv.dup, lv.nr
        low = (lanes(nr) & (2 * d - 1)) < d
        for j in range(lv.packs):
            m[j, 0:nr, :] = jnp.where(low, roll(pr[1, j, 0:nr, :], W - d), roll(pr[0, j, 0:nr, :], d))

    def side_halo(lv, r):
        m = v["m_%d" % r]
        d = lv.dup
        return lambda k, sp: roll(m[k // lv.per, 0 : lv.nr, :], W - d - 2 * d * ((k % lv.per) * lv.sp + sp))

    def row_halo(lv, r, sp):
        rr = v["rr_%d" % r]
        if lv is FINE:
            return [(rr[0, sp, k : k + 1, :], rr[1, sp, k : k + 1, :]) for k in range(10)]
        lo, hi = split(rr[0, sp]), split(rr[1, sp])
        return [(lo[k // 5][k % 5 : k % 5 + 1, :], hi[k // 5][k % 5 : k % 5 + 1, :]) for k in range(10)]

    def ring(nr, d, side, lo, hi):
        lane, row = lanes(nr), lax.broadcasted_iota(jnp.int32, (nr, W), 0)
        h = jnp.where((lane < d) | (lane >= W - d), side, 0.0)
        lo, hi = jnp.broadcast_to(lo, (nr, W)), jnp.broadcast_to(hi, (nr, W))
        return h + jnp.where(row == 0, lo, jnp.where(row == nr - 1, hi, 0.0))

    def inplane(lv, r, sp):
        side = side_halo(lv, r)
        rows = row_halo(lv, r, sp)
        return [ring(lv.nr, lv.dup, side(k, sp), *rows[k]) for k in range(10)]

    def beside(lv, r, q):
        axr = v["axr_%d" % r]
        if lv is FINE:
            return [axr[q, k] for k in range(10)]
        both = [split(axr[q, k, 0 : lv.nr, :]) for k in range(5)]
        return [w[0] for w in both] + [w[1] for w in both]

    def add(lv, tag, u, sp, pp, h):
        corr = smooth(lv, tag, sp, h)
        new = []
        for k in range(10):
            b = k * lv.npl + pp
            new.append(u[b, 8 : 8 + lv.nr, :] + corr[k])
            u[b, 8 : 8 + lv.nr, :] = new[k]
        return new

    def add_axial(lv, tag, u, r):
        for q in range(2 * lv.subs):
            a = 0 if q % 2 == 0 else lv.np - 1
            s = q // 2
            add(lv, tag, u, s * lv.np + a, s * lv.pad + 1 + a, beside(lv, r, q))

    def residual(lv, tag, u, sp, pp):
        f, c = v["f" + tag], v["c" + tag]
        d, nr = lv.dup, lv.nr
        lane = lanes(nr)
        xs, res = [], []
        for k in range(10):
            b = k * lv.npl + pp
            c0 = u[b, 8 : 8 + nr, :]
            y = f[k * lv.sp + sp, 0:nr, :] + (u[b + 1, 8 : 8 + nr, :] + u[b - 1, 8 : 8 + nr, :])
            y = y + (u[b, 7 : 7 + nr, :] + u[b, 9 : 9 + nr, :])
            y = y + (jnp.where(lane < d, 0.0, roll(c0, d)) + jnp.where(lane >= W - d, 0.0, roll(c0, W - d)))
            xs.append(c0)
            res.append(y)
        s = c[25 * lv.sp + sp, 0:nr, :]
        for i in range(5):
            re, im = res[i] + s * xs[5 + i], res[5 + i] - s * xs[i]
            for j in range(5):
                a = c[(5 * i + j) * lv.sp + sp, 0:nr, :]
                re = re - a * xs[j]
                im = im - a * xs[5 + j]
            res[i], res[5 + i] = re, im
        return xs, res

    def interior(lv, tag, u, new):
        def body(sp, pp):
            xs, res = residual(lv, tag, u, sp, pp)
            corr = smooth(lv, tag, sp, res)
            for k in range(10):
                new[k * lv.npl + pp, 8 : 8 + lv.nr, :] = xs[k] + corr[k]

        planes(lv, body)

    t = v["t"]

    def fold(lv, k, y):
        d, nr = lv.dup, lv.nr
        y = y + jnp.where((lanes(nr) & d) == 0, roll(y, W - d), roll(y, d))
        t[k, 0:nr, :] = y
        return t[k, pl.ds(0, nr // 2, stride=2), :] + t[k, pl.ds(1, nr // 2, stride=2), :]

    def send(lv, u, r, step=None):
        pack_inplane(lv, u, r, step)
        b = inplane_msgs(lv, r)
        for msg in b:
            msg.start()
        pack_axial(lv, u, r)
        a = axial_msgs(lv, r)
        for msg in a:
            msg.start()
        return a, b

    def recv(msgs):
        for msg in msgs:
            msg.recv()

    def finish(lv, tag, u, r, after=None):
        a, b = flying.pop(r)
        recv(a)
        add_axial(lv, tag, u, r)
        recv(b)
        turn(lv, r)
        step = lambda sp, pp: add(lv, tag, u, sp, pp, inplane(lv, r, sp))
        if after is None:
            planes(lv, lambda sp, pp: step(sp, pp) and None)
        else:
            flying[after] = send(lv, u, after, step)

    flying = {}
    ua, ub = v["ua0"], v["ub0"]
    f1, c1, c2 = v["f1"], v["c1"], v["c2"]

    for tag, lv in (("0", FINE), ("1", MID), ("2", COARSE)):
        for u in (v["ua" + tag], v["ub" + tag]):

            def clear(i, carry, u=u, lv=lv):
                u[i] = jnp.zeros((lv.height, W), F32)
                return carry

            lax.fori_loop(0, 10 * lv.npl, clear, 0)

    for c in loads[:3]:
        c.wait()
    coefficients(FINE, "0")
    first(FINE, "0", ua)

    pack_axial(FINE, ua, 0)
    count = sum(jnp.int32(1) if cond is None else cond.astype(jnp.int32) for _, cond in greet)
    pl.semaphore_wait(barrier, count)
    a0 = axial_msgs(FINE, 0)
    for msg in a0:
        msg.start()
    pack_inplane(FINE, ua, 0)
    b0 = inplane_msgs(FINE, 0)
    for msg in b0:
        msg.start()

    interior(FINE, "0", ua, ub)
    for c in loads[3:]:
        c.wait()

    def spread(cells_in):
        count, _, n = cells_in.shape
        pick = (
            lax.broadcasted_iota(jnp.int32, (n, W), 1) // (W // n) == lax.broadcasted_iota(jnp.int32, (n, W), 0)
        ).astype(F32)
        y = jnp.dot(
            cells_in.reshape(count * 8, n), pick, precision=lax.Precision.HIGHEST, preferred_element_type=F32
        )
        return y.reshape(count, 8, W)

    j1, j2, j2p = v["j1"], v["j2"], v["j2p"]
    c1s, c1r, c2s, c2r = v["c1s"], v["c1r"], v["c2s"], v["c2r"]

    def spread1(e, carry):
        y0, y1 = spread(j1[pl.ds(e * 4, 4)]), spread(j1[pl.ds((e + 13) * 4, 4)])
        c1[pl.ds(e * 8 + zh * 4, 4)] = y0
        c1[pl.ds((e + 13) * 8 + zh * 4, 4)] = y1
        for a in range(4):
            c1s[e * 4 + a] = join(y0[a], y1[a])
        return carry

    lax.fori_loop(0, 13, spread1, 0, unroll=13)

    def place2(e, carry):
        j2p[e, 0:4, :] = j2[2 * e]
        j2p[e, 4:8, :] = j2[2 * e + 1]
        return carry

    lax.fori_loop(0, 26, place2, 0, unroll=2)
    y2 = spread(j2p[...])
    for e in range(26):
        c2[e * 4 + zh * 2, 0:4, :] = y2[e, 0:4]
        c2[e * 4 + zh * 2 + 1, 0:4, :] = y2[e, 4:8]
    for e in range(13):
        c2s[e] = join(y2[e], y2[e + 13])

    recv(b0)
    mc1 = Msg(c1s, c1r, twin)
    mc2 = Msg(c2s, c2r, twin)
    mc1.start()
    mc2.start()
    turn(FINE, 0)
    planes(FINE, lambda sp, pp: add(FINE, "0", ub, sp, pp, inplane(FINE, 0, sp)) and None)
    recv(a0)
    add_axial(FINE, "0", ub, 0)

    for end in range(2):
        for k in range(5):
            pp = 1 if end == 0 else FINE.np
            part_s[end, k] = join(
                fold(FINE, k, ub[k * FINE.npl + pp, 8:24, :]),
                fold(FINE, 5 + k, ub[(5 + k) * FINE.npl + pp, 8:24, :]),
            )
    parts = [
        Msg(part_s.at[1], part_r.at[0], up, has_up, has_down),
        Msg(part_s.at[0], part_r.at[1], down, has_down, has_up),
    ]
    for msg in parts:
        msg.start()
    pack_inplane(FINE, ub, 1)
    b1 = inplane_msgs(FINE, 1)
    for msg in b1:
        msg.start()
    f_part = v["f_part"]

    def restrict0(a, carry):
        _, r0 = residual(FINE, "0", ub, 2 * a, 2 * a + 1)
        _, r1 = residual(FINE, "0", ub, 2 * a + 1, 2 * a + 2)
        for k in range(10):
            f_part[k * 4 + a] = 0.125 * fold(FINE, k, r0[k] + r1[k])
        return carry

    lax.fori_loop(0, 4, restrict0, 0)
    recv(b1)
    turn(FINE, 1)

    def restrict_halo0(a, carry):
        h0, h1 = inplane(FINE, 1, 2 * a), inplane(FINE, 1, 2 * a + 1)
        for k in range(10):
            f_part[k * 4 + a] = f_part[k * 4 + a] + 0.125 * fold(FINE, k, h0[k] + h1[k])
        return carry

    lax.fori_loop(0, 4, restrict_halo0, 0)
    recv(parts)
    gs, gr = v["gs"], v["gr"]
    for k in range(5):
        for end, a in ((0, 0), (1, 3)):
            re, im = split(part_r[end, k])
            f_part[k * 4 + a] = f_part[k * 4 + a] + 0.125 * re
            f_part[(5 + k) * 4 + a] = f_part[(5 + k) * 4 + a] + 0.125 * im
    for i in range(20):
        gs[i] = join(f_part[i], f_part[20 + i])
    mg = Msg(gs, gr, twin)
    mg.start()
    pack_axial(FINE, ub, 1)
    a1 = axial_msgs(FINE, 1)
    for msg in a1:
        msg.start()
    for k in range(10):
        f1[pl.ds(k * 8 + zh * 4, 4)] = f_part[k * 4 : k * 4 + 4]
    mc1.recv()
    mc2.recv()

    def split1(e, carry):
        for a in range(4):
            lo, hi = split(c1r[e * 4 + a])
            c1[e * 8 + (1 - zh) * 4 + a] = lo
            c1[(e + 13) * 8 + (1 - zh) * 4 + a] = hi
        lo, hi = split(c2r[e])
        for a in range(2):
            c2[e * 4 + (1 - zh) * 2 + a, 0:4, :] = lo[4 * a : 4 * a + 4]
            c2[(e + 13) * 4 + (1 - zh) * 2 + a, 0:4, :] = hi[4 * a : 4 * a + 4]
        return carry

    lax.fori_loop(0, 13, split1, 0)
    coefficients(MID, "1")
    coefficients(COARSE, "2")
    mg.recv()
    for i in range(20):
        re, im = split(gr[i])
        k, a = i // 4, i % 4
        f1[k * 8 + (1 - zh) * 4 + a] = re
        f1[(k + 5) * 8 + (1 - zh) * 4 + a] = im

    m_a, m_b = v["ua1"], v["ub1"]
    flying[2] = send(MID, m_a, 2, first_plane(MID, "1", m_a))
    interior(MID, "1", m_a, m_b)
    finish(MID, "1", m_b, 2, 3)
    f2 = v["f2"]
    for s in range(2):

        def restrict1(a, carry, s=s):
            _, r0 = residual(MID, "1", m_b, s * 4 + 2 * a, s * 6 + 2 * a + 1)
            _, r1 = residual(MID, "1", m_b, s * 4 + 2 * a + 1, s * 6 + 2 * a + 2)
            for k in range(10):
                f2[k * 4 + s * 2 + a, 0:4, :] = 0.125 * fold(MID, k, r0[k] + r1[k])
            return carry

        lax.fori_loop(0, 2, restrict1, 0)
    a3, b3 = flying.pop(3)
    recv(a3)
    recv(b3)
    turn(MID, 3)
    for s in range(2):
        for a in range(2):
            sp = s * 4 + 2 * a
            h0, h1, h2 = inplane(MID, 3, sp), inplane(MID, 3, sp + 1), beside(MID, 3, 2 * s + a)
            for k in range(10):
                i = k * 4 + s * 2 + a
                f2[i, 0:4, :] = f2[i, 0:4, :] + 0.125 * fold(MID, k, h0[k] + h1[k] + h2[k])

    q_a, q_b = v["ua2"], v["ub2"]
    flying[4] = send(COARSE, q_a, 4, first_plane(COARSE, "2", q_a))
    for r in range(4, 3 + COARSE_SWEEPS):
        interior(COARSE, "2", q_a, q_b)
        finish(COARSE, "2", q_b, r, r + 1 if r < 2 + COARSE_SWEEPS else None)
        q_a, q_b = q_b, q_a

    def prolong1(sp, pp):
        s, a = sp // 4, lax.rem(sp, 4)
        xs = []
        for k in range(10):
            w = q_a[k * COARSE.npl + s * 4 + 1 + a // 2, 8:16, :]
            t[k, pl.ds(0, 8, stride=2), :] = w
            t[k, pl.ds(1, 8, stride=2), :] = w
            b = k * MID.npl + pp
            xs.append(m_b[b, 8:16, :] + t[k, 0:8, :])
            m_b[b, 8:16, :] = xs[k]
        return xs

    flying[7] = send(MID, m_b, 7, prolong1)
    interior(MID, "1", m_b, m_a)
    finish(MID, "1", m_a, 7, 8)
    interior(MID, "1", m_a, m_b)
    finish(MID, "1", m_b, 8, 9)

    def double(k, w):
        t[k, pl.ds(0, 8, stride=2), :] = w
        t[k, pl.ds(1, 8, stride=2), :] = w
        return t[k, 0:16, :]

    def prolong0(a, carry):
        for k in range(10):
            w = m_b[k * MID.npl + zh * 6 + 1 + a // 2, 8:16, :]
            b = k * FINE.npl + 1 + a
            ub[b, 8:24, :] = ub[b, 8:24, :] + double(k, w)
        return carry

    lax.fori_loop(0, 8, prolong0, 0)
    interior(FINE, "0", ub, ua)
    planes(FINE, lambda sp, pp: add(FINE, "0", ua, sp, pp, inplane(FINE, 1, sp)) and None)
    recv(a1)
    add_axial(FINE, "0", ua, 1)
    a9, b9 = flying.pop(9)
    recv(a9)
    axr9 = v["axr_9"]
    for end, a in ((0, 0), (1, 7)):
        both = [split(axr9[2 * zh + end, k]) for k in range(5)]
        h = [w[0] for w in both] + [w[1] for w in both]
        add(FINE, "0", ua, a, a + 1, [double(k, h[k]) for k in range(10)])
    recv(b9)
    turn(MID, 9)
    side9 = side_halo(MID, 9)

    def add9(sp, pp):
        am = zh * 4 + sp // 2
        rows = row_halo(MID, 9, am)
        return add(FINE, "0", ua, sp, pp, [ring(16, 1, double(k, side9(k, am)), *rows[k]) for k in range(10)])

    planes(FINE, lambda sp, pp: add9(sp, pp) and None, 0, 8, 7)
    pack_axial(FINE, ua, 10)
    a10 = axial_msgs(FINE, 10)
    for msg in a10:
        msg.start()
    planes(FINE, lambda sp, pp: add9(sp, pp) and None, 1, 7)
    pack_inplane(FINE, ua, 10)
    b10 = inplane_msgs(FINE, 10)
    for msg in b10:
        msg.start()

    mask = v["mask"]
    interior(FINE, "0", ua, ub)
    recv(b10)
    turn(FINE, 10)

    def work(a, new):
        for k in range(10):
            out[k * 8 + a] = new[k]
        return mask[a].astype(F32) * (new[4] * new[6] - new[9] * new[1])

    def last(a, acc):
        return acc + work(a, add(FINE, "0", ub, a, a + 1, inplane(FINE, 10, a)))

    acc = lax.fori_loop(1, 7, last, jnp.zeros((16, W), F32))
    planes(FINE, lambda sp, pp: add(FINE, "0", ub, sp, pp, inplane(FINE, 10, sp)) and None, 0, 8, 7)
    recv(a10)
    for end, a in ((0, 0), (1, 7)):
        acc = acc + work(a, add(FINE, "0", ub, a, a + 1, beside(FINE, 10, end)))

    red0, red1 = v["red0"], v["red1"]
    mine0 = x * n_rad + rad
    red0[mine0] = acc[0:8] + acc[8:16]
    msgs = []
    n0 = nx * n_rad
    for off in range(1, n0):
        to = lax.rem(mine0 + off, n0)
        back = lax.rem(mine0 + n0 - off, n0)
        msgs.append(
            Msg(red0.at[mine0], red0.at[mine0], place(to // n_rad, lax.rem(to, n_rad), z, core), landing=red0.at[back])
        )
    for msg in msgs:
        msg.start()
    for msg in msgs:
        msg.recv()
    total = red0[0]
    for i in range(1, n0):
        total = total + red0[i]
    mine1 = z * 2 + core
    red1[mine1] = total
    msgs = []
    n1 = nz * 2
    for off in range(1, n1):
        to = lax.rem(mine1 + off, n1)
        back = lax.rem(mine1 + n1 - off, n1)
        msgs.append(Msg(red1.at[mine1], red1.at[mine1], place(x, rad, to // 2, lax.rem(to, 2)), landing=red1.at[back]))
    for msg in msgs:
        msg.start()
    for msg in msgs:
        msg.recv()
    total = red1[0]
    for i in range(1, n1):
        total = total + red1[i]
    damp[0, 0] = jnp.sum(total) * (25.0 / jnp.sqrt(jnp.float32(cells)))
    for msg in sent:
        when(msg.send_if, msg.copy.wait_send)


def solution(mesh):
    sizes = (mesh.shape["axial"], mesh.shape["radial"], mesh.shape["pitch"])

    def on_device(rhs, jac0, shift0, jac1, shift1, jac2, shift2, blade_mask):
        cells = shift0.size * sizes[0] * sizes[1] * sizes[2]
        shapes = scratch()
        out, damp = pl.pallas_call(
            functools.partial(kernel, sizes + (cells,), tuple(shapes)),
            out_shape=(jax.ShapeDtypeStruct((80, 16, W), F32), jax.ShapeDtypeStruct((1, 1), F32)),
            in_specs=[pl.BlockSpec(memory_space=pltpu.HBM)] * 8,
            out_specs=(pl.BlockSpec(memory_space=pltpu.VMEM), pl.BlockSpec(memory_space=pltpu.SMEM)),
            scratch_shapes=list(shapes.values()),
            compiler_params=pltpu.CompilerParams(
                collective_id=0, has_side_effects=True, vmem_limit_bytes=48 * 1024 * 1024
            ),
        )(
            *(
                pltpu.with_memory_space_constraint(a, pltpu.HBM)
                for a in (
                    rhs.reshape(80, 16, W),
                    jac0.reshape(200, 16, W),
                    shift0,
                    jac1.reshape(100, 8, 64),
                    shift1,
                    jac2.reshape(50, 4, 32),
                    shift2,
                    blade_mask,
                )
            )
        )
        return out.reshape(rhs.shape), damp.reshape(())

    spec = P(None, None, "axial", "radial", "pitch")
    flat = P("axial", "radial", "pitch")
    return jax.shard_map(
        on_device,
        mesh=mesh,
        in_specs=(spec, spec, flat, spec, flat, spec, flat, flat),
        out_specs=(spec, P()),
        check_vma=False,
    )
```

```python
import functools

import jax
import jax.numpy as jnp
from jax import lax
from jax.experimental import pallas as pl
from jax.experimental.pallas import tpu as pltpu
from jax.sharding import PartitionSpec as P

COARSE_SWEEPS = 4
MESH = pl.DeviceIdType.MESH
W = 128
F32 = jnp.float32


class Level:
    def __init__(self, rows, planes, subs, dup):
        self.nr, self.np, self.subs, self.dup = rows, planes, subs, dup
        self.sp = planes * subs
        self.pad = planes + 2
        self.npl = self.pad * subs
        self.nr8 = max(rows, 8)
        self.height = self.nr8 + 16
        self.per = 64 // (dup * self.sp)
        self.packs = -(-10 // self.per)


FINE = Level(16, 8, 1, 1)
MID = Level(8, 4, 2, 2)
COARSE = Level(4, 2, 2, 4)


def lanes(rows):
    return lax.broadcasted_iota(jnp.int32, (rows, W), 1)


def roll(x, shift):
    return pltpu.roll(x, shift, 1)


def join(a, b):
    return jnp.where((lanes(a.shape[0]) & 1) == 0, a, b)


def split(w):
    even = (lanes(w.shape[0]) & 1) == 0
    return jnp.where(even, w, roll(w, 1)), jnp.where(even, roll(w, W - 1), w)


def join2(a, b):
    return jnp.where((lanes(a.shape[0]) & 2) == 0, a, b)


def split2(w):
    low = (lanes(w.shape[0]) & 2) == 0
    return jnp.where(low, w, roll(w, 2)), jnp.where(low, roll(w, W - 2), w)


def scratch():
    shapes = {}

    def vmem(name, *shape):
        shapes[name] = pltpu.VMEM(shape, F32)

    for tag, lv in (("0", FINE), ("1", MID), ("2", COARSE)):
        vmem("ua" + tag, 10 * lv.npl, lv.height, W)
        vmem("ub" + tag, 10 * lv.npl, lv.height, W)
        vmem("f" + tag, 10 * lv.sp, lv.nr8, W)
        vmem("c" + tag, 26 * lv.sp, lv.nr8, W)
        vmem("sr" + tag, 5 * lv.sp, lv.nr8, W)
        vmem("si" + tag, 5 * lv.sp, lv.nr8, W)
    for r in range(ROUNDS):
        lv = LEVEL_OF[r]
        tag = "_%d" % r
        fields, ends = (10, 2) if lv is FINE else (5, 4)
        vmem("axs" + tag, ends, fields, lv.nr8, W)
        vmem("axr" + tag, ends, fields, lv.nr8, W)
        vmem("rs" + tag, 2, lv.sp, 16 if lv is FINE else 8, W)
        vmem("rr" + tag, 2, lv.sp, 16 if lv is FINE else 8, W)
        vmem("ps" + tag, lv.packs, lv.nr8, W)
        vmem("pr" + tag, 2, lv.packs, lv.nr8, W)
        vmem("m" + tag, lv.packs, lv.nr8, W)
    vmem("part_s", 2, 5, 8, W)
    vmem("part_r", 2, 5, 8, W)
    vmem("f_part", 40, 8, W)
    vmem("gs", 20, 8, W)
    vmem("gr", 20, 8, W)
    vmem("c1s", 52, 8, W)
    vmem("c1r", 52, 8, W)
    vmem("c2s", 7, 8, W)
    vmem("c2r", 7, 8, W)
    vmem("t", 10, 48, W)
    vmem("j1", 104, 8, 64)
    vmem("j2", 52, 4, 32)
    vmem("j2p", 26, 8, 32)
    vmem("red0", 16, 8, W)
    vmem("red1", 16, 8, W)
    shapes["mask"] = pltpu.VMEM((8, 16, W), jnp.int32)
    shapes["ss"] = pltpu.SemaphoreType.DMA((COPIES,))
    shapes["rs"] = pltpu.SemaphoreType.DMA((COPIES,))
    shapes["ls"] = pltpu.SemaphoreType.DMA((10,))
    return shapes


LEVEL_OF = [FINE, FINE, MID, MID, COARSE, COARSE, COARSE, MID, MID, MID, FINE]
ROUNDS = len(LEVEL_OF)
COPIES = 128
UNROLL = 2
SPLIT = 8


def kernel(sizes, names, *refs):
    rhs, jac0, shift0, jac1, shift1, jac2, shift2, blade = refs[:8]
    out, damp = refs[8:10]
    v = dict(zip(names, refs[10:]))
    n_ax, n_rad, n_pit, cells = sizes

    ax, rad, pit = lax.axis_index("axial"), lax.axis_index("radial"), lax.axis_index("pitch")
    core = lax.rem(ax, 2)
    zh = lax.rem(ax // 2, 2)
    x = ax // 4
    nx = n_ax // 4
    z = zh * n_pit + pit
    nz = 2 * n_pit

    def place(xx, yy, zz, cc):
        return {"axial": xx * 4 + (zz // n_pit) * 2 + cc, "radial": yy, "pitch": lax.rem(zz, n_pit)}

    up, down = {"axial": ax + 1}, {"axial": ax - 1}
    has_up, has_down = ax < n_ax - 1, ax > 0
    north, south = {"radial": rad + 1}, {"radial": rad - 1}
    has_north, has_south = rad < n_rad - 1, rad > 0
    east, west = {"pitch": lax.rem(pit + 1, n_pit)}, {"pitch": lax.rem(pit + n_pit - 1, n_pit)}
    z_east, z_west = place(x, rad, lax.rem(z + 1, nz), core), place(x, rad, lax.rem(z + nz - 1, nz), core)
    twin = {"axial": ax + 2 - 4 * zh}
    sibling = {"axial": ax + 1 - 2 * core}
    hop = {"axial": ax + 6 * core - 3}
    has_hop = jnp.logical_or(jnp.logical_and(core == 0, x > 0), jnp.logical_and(core == 1, x < nx - 1))
    wrap_e = pit == n_pit - 1
    wrap_w = pit == 0

    def when(cond, act):
        if cond is None:
            act()
        else:
            pl.when(cond)(act)

    local = [
        (rhs, v["f0"]),
        (jac0, v["c0"].at[pl.ds(0, 200)]),
        (shift0, v["c0"].at[pl.ds(200, 8)]),
        (jac1, v["j1"].at[pl.ds(0, 100)]),
        (shift1, v["j1"].at[pl.ds(100, 4)]),
        (jac2, v["j2"].at[pl.ds(0, 50)]),
        (shift2, v["j2"].at[pl.ds(50, 2)]),
        (blade, v["mask"]),
    ]
    loads = [pltpu.make_async_copy(a, b, v["ls"].at[i]) for i, (a, b) in enumerate(local)]
    for c in loads:
        c.start()

    barrier = pltpu.get_barrier_semaphore()
    greet = [
        (up, has_up),
        (down, has_down),
        (north, has_north),
        (south, has_south),
        (east, None),
        (west, None),
        (twin, None),
        (hop, has_hop),
        (z_east, wrap_e),
        (z_west, wrap_w),
    ]
    for dev, cond in greet:
        when(cond, lambda dev=dev: pl.semaphore_signal(barrier, inc=1, device_id=dev, device_id_type=MESH))

    counter = [0]
    sent = []

    class Msg:
        def __init__(self, src, dst, dev, send_if=None, recv_if=None, landing=None):
            i = counter[0]
            counter[0] += 1
            make = lambda d: pltpu.make_async_remote_copy(
                src_ref=src, dst_ref=d, send_sem=v["ss"].at[i], recv_sem=v["rs"].at[i], device_id=dev, device_id_type=MESH
            )
            self.copy = make(dst)
            self.into = self.copy if landing is None else make(landing)
            self.send_if, self.recv_if = send_if, recv_if

        def start(self):
            when(self.send_if, self.copy.start)
            sent.append(self)

        def recv(self):
            when(self.recv_if, self.into.wait_recv)

    for r in range(ROUNDS):
        tag = "_%d" % r
        axr, rr = v["axr" + tag], v["rr" + tag]

        def zero(ref, i):
            ref[i] = jnp.zeros(ref.shape[1:], F32)

        if LEVEL_OF[r] is FINE:
            when(jnp.logical_not(has_down), functools.partial(zero, axr, 0))
            when(jnp.logical_not(has_up), functools.partial(zero, axr, 1))
        else:
            when(jnp.logical_and(core == 0, x == 0), functools.partial(zero, axr, 0))
            when(jnp.logical_and(core == 1, x == nx - 1), functools.partial(zero, axr, 3))
        when(jnp.logical_not(has_south), functools.partial(zero, rr, 0))
        when(jnp.logical_not(has_north), functools.partial(zero, rr, 1))
    part_s, part_r = v["part_s"], v["part_r"]
    when(jnp.logical_not(has_down), lambda: zero(part_r, 0))
    when(jnp.logical_not(has_up), lambda: zero(part_r, 1))

    def planes(lv, body, lo=0, hi=None, step=1):
        hi = lv.np if hi is None else hi
        for s in range(lv.subs):

            def go(a, carry, s=s):
                a = lo + a * step
                body(s * lv.np + a, s * lv.pad + 1 + a)
                return carry

            lax.fori_loop(0, (hi - lo + step - 1) // step, go, 0)

    def coefficients(lv, tag):
        c, sr, si = v["c" + tag], v["sr" + tag], v["si" + tag]

        def body(sp, carry):
            s = c[25 * lv.sp + sp, 0 : lv.nr, :]
            for i in range(5):
                d = c[6 * i * lv.sp + sp, 0 : lv.nr, :]
                denom = d * d + s * s
                inv = 0.7 / jnp.where(denom > 0, denom, 1.0)
                sr[i * lv.sp + sp, 0 : lv.nr, :] = d * inv
                si[i * lv.sp + sp, 0 : lv.nr, :] = s * inv
            return carry

        lax.fori_loop(0, lv.sp, body, 0)

    def smooth(lv, tag, sp, res):
        sr, si = v["sr" + tag], v["si" + tag]
        new = [None] * 10
        for i in range(5):
            a, b = sr[i * lv.sp + sp, 0 : lv.nr, :], si[i * lv.sp + sp, 0 : lv.nr, :]
            new[i] = a * res[i] + b * res[5 + i]
            new[5 + i] = a * res[5 + i] - b * res[i]
        return new

    def first(lv, tag, u):
        step = first_plane(lv, tag, u)
        planes(lv, lambda sp, pp: step(sp, pp) and None)

    def first_plane(lv, tag, u):
        f = v["f" + tag]

        def step(sp, pp):
            new = smooth(lv, tag, sp, [f[k * lv.sp + sp, 0 : lv.nr, :] for k in range(10)])
            for k in range(10):
                u[k * lv.npl + pp, 8 : 8 + lv.nr, :] = new[k]
            return new

        return step

    def packing(lv):
        return tuple(jnp.zeros((lv.nr, W), F32) for _ in range(lv.packs))

    def pack_plane(lv, xs, sp, r, carry):
        rs = v["rs_%d" % r]
        d, nr = lv.dup, lv.nr
        group = lanes(nr) // (2 * d)
        packed = list(carry)
        for k in range(10):
            slot, j = (k % lv.per) * lv.sp + sp, k // lv.per
            packed[j] = jnp.where(group == slot, roll(xs[k], d + 2 * d * slot), packed[j])
        faces = xs if lv is FINE else [join(xs[k], xs[5 + k]) for k in range(5)]
        for k, w in enumerate(faces):
            rs[0, sp, k : k + 1, :] = w[0:1, :]
            rs[1, sp, k : k + 1, :] = w[nr - 1 : nr, :]
        return tuple(packed)

    def pack_inplane(lv, u, r, step=None):
        ps = v["ps_%d" % r]
        carry = packing(lv)
        for s in range(lv.subs):

            def body(a, carry, s=s):
                sp, pp = s * lv.np + a, s * lv.pad + 1 + a
                if step is None:
                    xs = [u[k * lv.npl + pp, 8 : 8 + lv.nr, :] for k in range(10)]
                else:
                    xs = step(sp, pp)
                return pack_plane(lv, xs, sp, r, carry)

            carry = lax.fori_loop(0, lv.np, body, carry, unroll=UNROLL if lv is not FINE else 2)
        for j in range(lv.packs):
            ps[j, 0 : lv.nr, :] = carry[j]

    def inplane_msgs(lv, r):
        tag = "_%d" % r
        rs, rr, ps, pr = (v[n + tag] for n in ("rs", "rr", "ps", "pr"))
        e, w = (east, west) if lv is FINE else (z_east, z_west)
        return [
            Msg(ps, pr.at[0], e),
            Msg(ps, pr.at[1], w),
            Msg(rs.at[1], rr.at[0], north, has_north, has_south),
            Msg(rs.at[0], rr.at[1], south, has_south, has_north),
        ]

    def pack_axial(lv, u, r):
        axs = v["axs_%d" % r]
        nr = lv.nr
        if lv is FINE:

            def body(k, carry):
                axs[0, k] = u[k * lv.npl + 1, 8 : 8 + nr, :]
                axs[1, k] = u[k * lv.npl + lv.np, 8 : 8 + nr, :]
                return carry

            lax.fori_loop(0, 10, body, 0)
            return
        for q in range(4):
            pp = (q // 2) * lv.pad + (1 if q % 2 == 0 else lv.np)
            for k in range(5):
                axs[q, k, 0:nr, :] = join(
                    u[k * lv.npl + pp, 8 : 8 + nr, :], u[(5 + k) * lv.npl + pp, 8 : 8 + nr, :]
                )

    def axial_msgs(lv, r):
        axs, axr = v["axs_%d" % r], v["axr_%d" % r]
        if lv is FINE:
            return [
                Msg(axs.at[1], axr.at[0], up, has_up, has_down),
                Msg(axs.at[0], axr.at[1], down, has_down, has_up),
            ]
        return [
            Msg(axs.at[3 * core], axr.at[3 - 3 * core], hop, has_hop, has_hop, landing=axr.at[3 * core]),
            Msg(axs.at[pl.ds(1 - core, 3)], axr.at[pl.ds(core, 3)], sibling, landing=axr.at[pl.ds(1 - core, 3)]),
        ]

    def turn(lv, r):
        pr, m = v["pr_%d" % r], v["m_%d" % r]
        d, nr = lv.dup, lv.nr
        low = (lanes(nr) & (2 * d - 1)) < d
        for j in range(lv.packs):
            m[j, 0:nr, :] = jnp.where(low, roll(pr[1, j, 0:nr, :], W - d), roll(pr[0, j, 0:nr, :], d))

    def side_halo(lv, r):
        m = v["m_%d" % r]
        d = lv.dup
        return lambda k, sp: roll(m[k // lv.per, 0 : lv.nr, :], W - d - 2 * d * ((k % lv.per) * lv.sp + sp))

    def row_halo(lv, r, sp):
        rr = v["rr_%d" % r]
        if lv is FINE:
            return [(rr[0, sp, k : k + 1, :], rr[1, sp, k : k + 1, :]) for k in range(10)]
        lo, hi = split(rr[0, sp]), split(rr[1, sp])
        return [(lo[k // 5][k % 5 : k % 5 + 1, :], hi[k // 5][k % 5 : k % 5 + 1, :]) for k in range(10)]

    def ring(nr, d, side, lo, hi):
        lane, row = lanes(nr), lax.broadcasted_iota(jnp.int32, (nr, W), 0)
        h = jnp.where((lane < d) | (lane >= W - d), side, 0.0)
        lo, hi = jnp.broadcast_to(lo, (nr, W)), jnp.broadcast_to(hi, (nr, W))
        return h + jnp.where(row == 0, lo, jnp.where(row == nr - 1, hi, 0.0))

    def inplane(lv, r, sp):
        side = side_halo(lv, r)
        rows = row_halo(lv, r, sp)
        return [ring(lv.nr, lv.dup, side(k, sp), *rows[k]) for k in range(10)]

    def beside(lv, r, q):
        axr = v["axr_%d" % r]
        if lv is FINE:
            return [axr[q, k] for k in range(10)]
        both = [split(axr[q, k, 0 : lv.nr, :]) for k in range(5)]
        return [w[0] for w in both] + [w[1] for w in both]

    def add(lv, tag, u, sp, pp, h):
        corr = smooth(lv, tag, sp, h)
        new = []
        for k in range(10):
            b = k * lv.npl + pp
            new.append(u[b, 8 : 8 + lv.nr, :] + corr[k])
            u[b, 8 : 8 + lv.nr, :] = new[k]
        return new

    def add_axial(lv, tag, u, r):
        for q in range(2 * lv.subs):
            a = 0 if q % 2 == 0 else lv.np - 1
            s = q // 2
            add(lv, tag, u, s * lv.np + a, s * lv.pad + 1 + a, beside(lv, r, q))

    def residual(lv, tag, u, sp, pp):
        f, c = v["f" + tag], v["c" + tag]
        d, nr = lv.dup, lv.nr
        lane = lanes(nr)
        xs, res = [], []
        for k in range(10):
            b = k * lv.npl + pp
            c0 = u[b, 8 : 8 + nr, :]
            y = f[k * lv.sp + sp, 0:nr, :] + (u[b + 1, 8 : 8 + nr, :] + u[b - 1, 8 : 8 + nr, :])
            y = y + (u[b, 7 : 7 + nr, :] + u[b, 9 : 9 + nr, :])
            y = y + (jnp.where(lane < d, 0.0, roll(c0, d)) + jnp.where(lane >= W - d, 0.0, roll(c0, W - d)))
            xs.append(c0)
            res.append(y)
        s = c[25 * lv.sp + sp, 0:nr, :]
        for i in range(5):
            re, im = res[i] + s * xs[5 + i], res[5 + i] - s * xs[i]
            for j in range(5):
                a = c[(5 * i + j) * lv.sp + sp, 0:nr, :]
                re = re - a * xs[j]
                im = im - a * xs[5 + j]
            res[i], res[5 + i] = re, im
        return xs, res

    def interior(lv, tag, u, new):
        def body(sp, pp):
            xs, res = residual(lv, tag, u, sp, pp)
            corr = smooth(lv, tag, sp, res)
            for k in range(10):
                new[k * lv.npl + pp, 8 : 8 + lv.nr, :] = xs[k] + corr[k]

        planes(lv, body)

    t = v["t"]

    def fold(lv, k, y):
        d, nr = lv.dup, lv.nr
        y = y + jnp.where((lanes(nr) & d) == 0, roll(y, W - d), roll(y, d))
        t[k, 0:nr, :] = y
        return t[k, pl.ds(0, nr // 2, stride=2), :] + t[k, pl.ds(1, nr // 2, stride=2), :]

    def send(lv, u, r, step=None):
        pack_inplane(lv, u, r, step)
        b = inplane_msgs(lv, r)
        for msg in b:
            msg.start()
        pack_axial(lv, u, r)
        a = axial_msgs(lv, r)
        for msg in a:
            msg.start()
        return a, b

    def recv(msgs):
        for msg in msgs:
            msg.recv()

    def finish(lv, tag, u, r, after=None):
        a, b = flying.pop(r)
        recv(a)
        add_axial(lv, tag, u, r)
        recv(b)
        turn(lv, r)
        step = lambda sp, pp: add(lv, tag, u, sp, pp, inplane(lv, r, sp))
        if after is None:
            planes(lv, lambda sp, pp: step(sp, pp) and None)
        else:
            flying[after] = send(lv, u, after, step)

    flying = {}
    ua, ub = v["ua0"], v["ub0"]
    f1, c1, c2 = v["f1"], v["c1"], v["c2"]

    for tag, lv in (("0", FINE), ("1", MID), ("2", COARSE)):
        for u in (v["ua" + tag], v["ub" + tag]):

            def clear(i, carry, u=u, lv=lv):
                u[i] = jnp.zeros((lv.height, W), F32)
                return carry

            lax.fori_loop(0, 10 * lv.npl, clear, 0)

    for c in loads[:3]:
        c.wait()
    coefficients(FINE, "0")
    first(FINE, "0", ua)

    pack_axial(FINE, ua, 0)
    count = sum(jnp.int32(1) if cond is None else cond.astype(jnp.int32) for _, cond in greet)
    pl.semaphore_wait(barrier, count)
    a0 = axial_msgs(FINE, 0)
    for msg in a0:
        msg.start()
    pack_inplane(FINE, ua, 0)
    b0 = inplane_msgs(FINE, 0)
    for msg in b0:
        msg.start()

    for c in loads[3:]:
        c.wait()

    def spread(cells_in):
        count, _, n = cells_in.shape
        pick = (
            lax.broadcasted_iota(jnp.int32, (n, W), 1) // (W // n) == lax.broadcasted_iota(jnp.int32, (n, W), 0)
        ).astype(F32)
        y = jnp.dot(
            cells_in.reshape(count * 8, n), pick, precision=lax.Precision.HIGHEST, preferred_element_type=F32
        )
        return y.reshape(count, 8, W)

    j1, j2, j2p = v["j1"], v["j2"], v["j2p"]
    c1s, c1r, c2s, c2r = v["c1s"], v["c1r"], v["c2s"], v["c2r"]

    def spread1(e, carry):
        y0, y1 = spread(j1[pl.ds(e * 4, 4)]), spread(j1[pl.ds((e + 13) * 4, 4)])
        c1[pl.ds(e * 8 + zh * 4, 4)] = y0
        c1[pl.ds((e + 13) * 8 + zh * 4, 4)] = y1
        for a in range(4):
            c1s[e * 4 + a] = join(y0[a], y1[a])
        return carry

    lax.fori_loop(0, 13, spread1, 0, unroll=13)

    def place2(e, carry):
        j2p[e, 0:4, :] = j2[2 * e]
        j2p[e, 4:8, :] = j2[2 * e + 1]
        return carry

    lax.fori_loop(0, 26, place2, 0, unroll=2)
    y2 = spread(j2p[...])
    for e in range(26):
        c2[e * 4 + zh * 2, 0:4, :] = y2[e, 0:4]
        c2[e * 4 + zh * 2 + 1, 0:4, :] = y2[e, 4:8]
    for e in range(7):
        c2s[e] = join2(join(y2[e], y2[e + 7]), join(y2[e + 14], y2[min(e + 21, 25)]))
    first_part, rest = pl.ds(0, SPLIT), pl.ds(SPLIT, 52 - SPLIT)
    mc = [
        Msg(c1s.at[first_part], c1r.at[first_part], twin),
        Msg(c1s.at[rest], c1r.at[rest], twin),
        Msg(c2s, c2r, twin),
    ]
    mc[0].start()
    interior(FINE, "0", ua, ub)

    recv(b0)
    turn(FINE, 0)
    planes(FINE, lambda sp, pp: add(FINE, "0", ub, sp, pp, inplane(FINE, 0, sp)) and None)
    recv(a0)
    add_axial(FINE, "0", ub, 0)

    for end in range(2):
        for k in range(5):
            pp = 1 if end == 0 else FINE.np
            part_s[end, k] = join(
                fold(FINE, k, ub[k * FINE.npl + pp, 8:24, :]),
                fold(FINE, 5 + k, ub[(5 + k) * FINE.npl + pp, 8:24, :]),
            )
    parts = [
        Msg(part_s.at[1], part_r.at[0], up, has_up, has_down),
        Msg(part_s.at[0], part_r.at[1], down, has_down, has_up),
    ]
    for msg in parts:
        msg.start()
    pack_inplane(FINE, ub, 1)
    b1 = inplane_msgs(FINE, 1)
    for msg in b1:
        msg.start()
    for msg in mc[1:]:
        msg.start()
    f_part = v["f_part"]

    def restrict0(a, carry):
        _, r0 = residual(FINE, "0", ub, 2 * a, 2 * a + 1)
        _, r1 = residual(FINE, "0", ub, 2 * a + 1, 2 * a + 2)
        for k in range(10):
            f_part[k * 4 + a] = 0.125 * fold(FINE, k, r0[k] + r1[k])
        return carry

    lax.fori_loop(0, 4, restrict0, 0)
    recv(b1)
    turn(FINE, 1)

    def restrict_halo0(a, carry):
        h0, h1 = inplane(FINE, 1, 2 * a), inplane(FINE, 1, 2 * a + 1)
        for k in range(10):
            f_part[k * 4 + a] = f_part[k * 4 + a] + 0.125 * fold(FINE, k, h0[k] + h1[k])
        return carry

    lax.fori_loop(0, 4, restrict_halo0, 0)
    recv(parts)
    gs, gr = v["gs"], v["gr"]
    for k in range(5):
        for end, a in ((0, 0), (1, 3)):
            re, im = split(part_r[end, k])
            f_part[k * 4 + a] = f_part[k * 4 + a] + 0.125 * re
            f_part[(5 + k) * 4 + a] = f_part[(5 + k) * 4 + a] + 0.125 * im
    for i in range(20):
        gs[i] = join(f_part[i], f_part[20 + i])
    mg = Msg(gs, gr, twin)
    mg.start()
    pack_axial(FINE, ub, 1)
    for k in range(10):
        f1[pl.ds(k * 8 + zh * 4, 4)] = f_part[k * 4 : k * 4 + 4]
    recv(mc)

    def split1(e, carry):
        for a in range(4):
            lo, hi = split(c1r[e * 4 + a])
            c1[e * 8 + (1 - zh) * 4 + a] = lo
            c1[(e + 13) * 8 + (1 - zh) * 4 + a] = hi
        return carry

    lax.fori_loop(0, 13, split1, 0, unroll=2)
    for e in range(7):
        low, high = split2(c2r[e])
        for i, y in enumerate(split(low) + split(high)):
            if e + 7 * i < 26:
                for a in range(2):
                    c2[(e + 7 * i) * 4 + (1 - zh) * 2 + a, 0:4, :] = y[4 * a : 4 * a + 4]
    coefficients(MID, "1")
    coefficients(COARSE, "2")
    mg.recv()
    for i in range(20):
        re, im = split(gr[i])
        k, a = i // 4, i % 4
        f1[k * 8 + (1 - zh) * 4 + a] = re
        f1[(k + 5) * 8 + (1 - zh) * 4 + a] = im

    m_a, m_b = v["ua1"], v["ub1"]
    flying[2] = send(MID, m_a, 2, first_plane(MID, "1", m_a))
    axs1, axr1 = v["axs_1"], v["axr_1"]
    a1 = []

    def piece():
        two = pl.ds(len(a1), 2)
        for dst, dev, there, here in ((0, up, has_up, has_down), (1, down, has_down, has_up)):
            msg = Msg(axs1.at[1 - dst, two], axr1.at[dst, two], dev, there, here)
            msg.start()
            a1.append(msg)

    piece()
    interior(MID, "1", m_a, m_b)
    finish(MID, "1", m_b, 2, 3)
    piece()
    f2 = v["f2"]
    for s in range(2):

        def restrict1(a, carry, s=s):
            _, r0 = residual(MID, "1", m_b, s * 4 + 2 * a, s * 6 + 2 * a + 1)
            _, r1 = residual(MID, "1", m_b, s * 4 + 2 * a + 1, s * 6 + 2 * a + 2)
            for k in range(10):
                f2[k * 4 + s * 2 + a, 0:4, :] = 0.125 * fold(MID, k, r0[k] + r1[k])
            return carry

        lax.fori_loop(0, 2, restrict1, 0)
    a3, b3 = flying.pop(3)
    recv(a3)
    recv(b3)
    turn(MID, 3)
    for s in range(2):
        for a in range(2):
            sp = s * 4 + 2 * a
            h0, h1, h2 = inplane(MID, 3, sp), inplane(MID, 3, sp + 1), beside(MID, 3, 2 * s + a)
            for k in range(10):
                i = k * 4 + s * 2 + a
                f2[i, 0:4, :] = f2[i, 0:4, :] + 0.125 * fold(MID, k, h0[k] + h1[k] + h2[k])

    q_a, q_b = v["ua2"], v["ub2"]
    flying[4] = send(COARSE, q_a, 4, first_plane(COARSE, "2", q_a))
    for r in range(4, 3 + COARSE_SWEEPS):
        piece()
        interior(COARSE, "2", q_a, q_b)
        finish(COARSE, "2", q_b, r, r + 1 if r < 2 + COARSE_SWEEPS else None)
        q_a, q_b = q_b, q_a

    def prolong1(sp, pp):
        s, a = sp // 4, lax.rem(sp, 4)
        xs = []
        for k in range(10):
            w = q_a[k * COARSE.npl + s * 4 + 1 + a // 2, 8:16, :]
            t[k, pl.ds(0, 8, stride=2), :] = w
            t[k, pl.ds(1, 8, stride=2), :] = w
            b = k * MID.npl + pp
            xs.append(m_b[b, 8:16, :] + t[k, 0:8, :])
            m_b[b, 8:16, :] = xs[k]
        return xs

    flying[7] = send(MID, m_b, 7, prolong1)
    interior(MID, "1", m_b, m_a)
    finish(MID, "1", m_a, 7, 8)
    interior(MID, "1", m_a, m_b)
    finish(MID, "1", m_b, 8, 9)

    def double(k, w):
        t[k, pl.ds(0, 8, stride=2), :] = w
        t[k, pl.ds(1, 8, stride=2), :] = w
        return t[k, 0:16, :]

    def prolong0(a, carry):
        for k in range(10):
            w = m_b[k * MID.npl + zh * 6 + 1 + a // 2, 8:16, :]
            b = k * FINE.npl + 1 + a
            ub[b, 8:24, :] = ub[b, 8:24, :] + double(k, w)
        return carry

    lax.fori_loop(0, 8, prolong0, 0)
    interior(FINE, "0", ub, ua)
    planes(FINE, lambda sp, pp: add(FINE, "0", ua, sp, pp, inplane(FINE, 1, sp)) and None)
    recv(a1)
    add_axial(FINE, "0", ua, 1)
    a9, b9 = flying.pop(9)
    recv(a9)
    axr9 = v["axr_9"]
    for end, a in ((0, 0), (1, 7)):
        both = [split(axr9[2 * zh + end, k]) for k in range(5)]
        h = [w[0] for w in both] + [w[1] for w in both]
        add(FINE, "0", ua, a, a + 1, [double(k, h[k]) for k in range(10)])
    recv(b9)
    turn(MID, 9)
    side9 = side_halo(MID, 9)

    def add9(sp, pp):
        am = zh * 4 + sp // 2
        rows = row_halo(MID, 9, am)
        return add(FINE, "0", ua, sp, pp, [ring(16, 1, double(k, side9(k, am)), *rows[k]) for k in range(10)])

    planes(FINE, lambda sp, pp: add9(sp, pp) and None, 0, 8, 7)
    pack_axial(FINE, ua, 10)
    a10 = axial_msgs(FINE, 10)
    for msg in a10:
        msg.start()
    planes(FINE, lambda sp, pp: add9(sp, pp) and None, 1, 7)
    pack_inplane(FINE, ua, 10)
    b10 = inplane_msgs(FINE, 10)
    for msg in b10:
        msg.start()

    mask = v["mask"]
    interior(FINE, "0", ua, ub)
    recv(b10)
    turn(FINE, 10)

    def work(a, new):
        for k in range(10):
            out[k * 8 + a] = new[k]
        return mask[a].astype(F32) * (new[4] * new[6] - new[9] * new[1])

    def last(a, acc):
        return acc + work(a, add(FINE, "0", ub, a, a + 1, inplane(FINE, 10, a)))

    acc = lax.fori_loop(1, 7, last, jnp.zeros((16, W), F32))
    planes(FINE, lambda sp, pp: add(FINE, "0", ub, sp, pp, inplane(FINE, 10, sp)) and None, 0, 8, 7)
    recv(a10)
    for end, a in ((0, 0), (1, 7)):
        acc = acc + work(a, add(FINE, "0", ub, a, a + 1, beside(FINE, 10, end)))

    def total(buf, group, value):
        mine, count, members = group
        buf[mine] = value
        msgs = [Msg(buf.at[mine], buf.at[mine], dev, landing=buf.at[slot]) for dev, slot in members]
        earlier = list(sent)
        sent.clear()
        for msg in msgs:
            msg.start()
        for msg in earlier:
            when(msg.send_if, msg.copy.wait_send)
        recv(msgs)
        parts = [buf[i] for i in range(count)]
        while len(parts) > 1:
            parts = [p + q for p, q in zip(parts[::2], parts[1::2])] + parts[len(parts) - len(parts) % 2 :]
        return parts[0]

    def offsets(*counts):
        far = lambda o: sum(min(d, n - d) for d, n in zip(o, counts))
        every = [(i, j) for i in range(counts[0]) for j in range(counts[1])]
        return sorted(every[1:], key=lambda o: -far(o))

    across = []
    for i, j in offsets(nx, n_rad):
        there = lambda sign: (lax.rem(x + sign * i + nx, nx), lax.rem(rad + sign * j + n_rad, n_rad))
        (tx, ty), (fx, fy) = there(1), there(-1)
        across.append((place(tx, ty, z, core), fx * n_rad + fy))
    along = []
    for i, j in offsets(nz, 2):
        tz, fz = lax.rem(z + i, nz), lax.rem(z + nz - i, nz)
        other = core if j == 0 else 1 - core
        along.append((place(x, rad, tz, other), fz * 2 + other))
    sum_xy = total(v["red0"], (x * n_rad + rad, nx * n_rad, across), acc[0:8] + acc[8:16])
    sum_all = total(v["red1"], (z * 2 + core, nz * 2, along), sum_xy)
    damp[0, 0] = jnp.sum(sum_all) * (25.0 / jnp.sqrt(jnp.float32(cells)))
    for msg in sent:
        when(msg.send_if, msg.copy.wait_send)


def solution(mesh):
    sizes = (mesh.shape["axial"], mesh.shape["radial"], mesh.shape["pitch"])

    def on_device(rhs, jac0, shift0, jac1, shift1, jac2, shift2, blade_mask):
        cells = shift0.size * sizes[0] * sizes[1] * sizes[2]
        shapes = scratch()
        out, damp = pl.pallas_call(
            functools.partial(kernel, sizes + (cells,), tuple(shapes)),
            out_shape=(jax.ShapeDtypeStruct((80, 16, W), F32), jax.ShapeDtypeStruct((1, 1), F32)),
            in_specs=[pl.BlockSpec(memory_space=pltpu.HBM)] * 8,
            out_specs=(pl.BlockSpec(memory_space=pltpu.VMEM), pl.BlockSpec(memory_space=pltpu.SMEM)),
            scratch_shapes=list(shapes.values()),
            compiler_params=pltpu.CompilerParams(
                collective_id=0, has_side_effects=True, vmem_limit_bytes=48 * 1024 * 1024
            ),
        )(
            *(
                pltpu.with_memory_space_constraint(a, pltpu.HBM)
                for a in (
                    rhs.reshape(80, 16, W),
                    jac0.reshape(200, 16, W),
                    shift0,
                    jac1.reshape(100, 8, 64),
                    shift1,
                    jac2.reshape(50, 4, 32),
                    shift2,
                    blade_mask,
                )
            )
        )
        return out.reshape(rhs.shape), damp.reshape(())

    spec = P(None, None, "axial", "radial", "pitch")
    flat = P("axial", "radial", "pitch")
    return jax.shard_map(
        on_device,
        mesh=mesh,
        in_specs=(spec, spec, flat, spec, flat, spec, flat, flat),
        out_specs=(spec, P()),
        check_vma=False,
    )
```

```python
import functools

import jax
import jax.numpy as jnp
from jax import lax
from jax.experimental import pallas as pl
from jax.experimental.pallas import tpu as pltpu
from jax.sharding import PartitionSpec as P

COARSE_SWEEPS = 4
MESH = pl.DeviceIdType.MESH
W = 128
F32 = jnp.float32


class Level:
    def __init__(self, rows, planes, subs, dup):
        self.nr, self.np, self.subs, self.dup = rows, planes, subs, dup
        self.sp = planes * subs
        self.pad = planes + 2
        self.npl = self.pad * subs
        self.nr8 = max(rows, 8)
        self.height = self.nr8 + 16
        self.per = 64 // (dup * self.sp)
        self.packs = -(-10 // self.per)


FINE = Level(16, 8, 1, 1)
MID = Level(8, 4, 2, 2)
COARSE = Level(4, 2, 2, 4)


def lanes(rows):
    return lax.broadcasted_iota(jnp.int32, (rows, W), 1)


def roll(x, shift):
    return pltpu.roll(x, shift, 1)


def join(a, b):
    return jnp.where((lanes(a.shape[0]) & 1) == 0, a, b)


def split(w):
    even = (lanes(w.shape[0]) & 1) == 0
    return jnp.where(even, w, roll(w, 1)), jnp.where(even, roll(w, W - 1), w)


def join2(a, b):
    return jnp.where((lanes(a.shape[0]) & 2) == 0, a, b)


def split2(w):
    low = (lanes(w.shape[0]) & 2) == 0
    return jnp.where(low, w, roll(w, 2)), jnp.where(low, roll(w, W - 2), w)


def scratch():
    shapes = {}

    def vmem(name, *shape):
        shapes[name] = pltpu.VMEM(shape, F32)

    for tag, lv in (("0", FINE), ("1", MID), ("2", COARSE)):
        vmem("ua" + tag, 10 * lv.npl, lv.height, W)
        vmem("ub" + tag, 10 * lv.npl, lv.height, W)
        vmem("f" + tag, 10 * lv.sp, lv.nr8, W)
        vmem("c" + tag, 26 * lv.sp, lv.nr8, W)
        vmem("sr" + tag, 5 * lv.sp, lv.nr8, W)
        vmem("si" + tag, 5 * lv.sp, lv.nr8, W)
    for r in range(ROUNDS):
        lv = LEVEL_OF[r]
        tag = "_%d" % r
        fields, ends = (10, 2) if lv is FINE else (5, 4)
        vmem("axs" + tag, ends, fields, lv.nr8, W)
        vmem("axr" + tag, ends, fields, lv.nr8, W)
        vmem("rs" + tag, 2, lv.sp, 16 if lv is FINE else 8, W)
        vmem("rr" + tag, 2, lv.sp, 16 if lv is FINE else 8, W)
        vmem("ps" + tag, lv.packs, lv.nr8, W)
        vmem("pr" + tag, 2, lv.packs, lv.nr8, W)
        vmem("m" + tag, lv.packs, lv.nr8, W)
    vmem("part_s", 2, 5, 8, W)
    vmem("part_r", 2, 5, 8, W)
    vmem("f_part", 40, 8, W)
    vmem("gs", 20, 8, W)
    vmem("gr", 20, 8, W)
    vmem("c1s", 52, 8, W)
    vmem("c1r", 52, 8, W)
    vmem("c2s", 7, 8, W)
    vmem("c2r", 7, 8, W)
    vmem("t", 10, 48, W)
    vmem("j1", 104, 8, 64)
    vmem("j2", 52, 4, 32)
    vmem("j2p", 26, 8, 32)
    vmem("red0", 16, 8, W)
    vmem("red1", 16, 8, W)
    shapes["mask"] = pltpu.VMEM((8, 16, W), jnp.int32)
    shapes["ss"] = pltpu.SemaphoreType.DMA((COPIES,))
    shapes["rs"] = pltpu.SemaphoreType.DMA((COPIES,))
    shapes["ls"] = pltpu.SemaphoreType.DMA((16,))
    return shapes


LEVEL_OF = [FINE, FINE, MID, MID, COARSE, COARSE, COARSE, MID, MID, MID, FINE]
ROUNDS = len(LEVEL_OF)
COPIES = 128
UNROLL = 4
SPLIT = 20


def kernel(sizes, names, *refs):
    rhs, jac0, shift0, jac1, shift1, jac2, shift2, blade = refs[:8]
    out, damp = refs[8:10]
    v = dict(zip(names, refs[10:]))
    n_ax, n_rad, n_pit, cells = sizes

    ax, rad, pit = lax.axis_index("axial"), lax.axis_index("radial"), lax.axis_index("pitch")
    core = lax.rem(ax, 2)
    zh = lax.rem(ax // 2, 2)
    x = ax // 4
    nx = n_ax // 4
    z = zh * n_pit + pit
    nz = 2 * n_pit

    def place(xx, yy, zz, cc):
        return {"axial": xx * 4 + (zz // n_pit) * 2 + cc, "radial": yy, "pitch": lax.rem(zz, n_pit)}

    up, down = {"axial": ax + 1}, {"axial": ax - 1}
    has_up, has_down = ax < n_ax - 1, ax > 0
    north, south = {"radial": rad + 1}, {"radial": rad - 1}
    has_north, has_south = rad < n_rad - 1, rad > 0
    east, west = {"pitch": lax.rem(pit + 1, n_pit)}, {"pitch": lax.rem(pit + n_pit - 1, n_pit)}
    z_east, z_west = place(x, rad, lax.rem(z + 1, nz), core), place(x, rad, lax.rem(z + nz - 1, nz), core)
    twin = {"axial": ax + 2 - 4 * zh}
    sibling = {"axial": ax + 1 - 2 * core}
    hop = {"axial": ax + 6 * core - 3}
    has_hop = jnp.logical_or(jnp.logical_and(core == 0, x > 0), jnp.logical_and(core == 1, x < nx - 1))
    wrap_e = pit == n_pit - 1
    wrap_w = pit == 0

    def when(cond, act):
        if cond is None:
            act()
        else:
            pl.when(cond)(act)

    local = [
        (rhs, v["f0"]),
        (shift0, v["c0"].at[pl.ds(200, 8)]),
        *((jac0.at[pl.ds(48 * i, 8)], v["c0"].at[pl.ds(48 * i, 8)]) for i in range(5)),
        *((jac0.at[pl.ds(48 * i + 8, 40)], v["c0"].at[pl.ds(48 * i + 8, 40)]) for i in range(4)),
        (jac1, v["j1"].at[pl.ds(0, 100)]),
        (shift1, v["j1"].at[pl.ds(100, 4)]),
        (jac2, v["j2"].at[pl.ds(0, 50)]),
        (shift2, v["j2"].at[pl.ds(50, 2)]),
        (blade, v["mask"]),
    ]
    loads = [pltpu.make_async_copy(a, b, v["ls"].at[i]) for i, (a, b) in enumerate(local)]
    for c in loads:
        c.start()

    barrier = pltpu.get_barrier_semaphore()
    greet = [
        (up, has_up),
        (down, has_down),
        (north, has_north),
        (south, has_south),
        (east, None),
        (west, None),
        (twin, None),
        (hop, has_hop),
        (z_east, wrap_e),
        (z_west, wrap_w),
    ]
    for dev, cond in greet:
        when(cond, lambda dev=dev: pl.semaphore_signal(barrier, inc=1, device_id=dev, device_id_type=MESH))

    counter = [0]
    sent = []

    class Msg:
        def __init__(self, src, dst, dev, send_if=None, recv_if=None, landing=None):
            i = counter[0]
            counter[0] += 1
            make = lambda d: pltpu.make_async_remote_copy(
                src_ref=src, dst_ref=d, send_sem=v["ss"].at[i], recv_sem=v["rs"].at[i], device_id=dev, device_id_type=MESH
            )
            self.copy = make(dst)
            self.into = self.copy if landing is None else make(landing)
            self.send_if, self.recv_if = send_if, recv_if

        def start(self):
            when(self.send_if, self.copy.start)
            sent.append(self)

        def recv(self):
            when(self.recv_if, self.into.wait_recv)

    for r in range(ROUNDS):
        tag = "_%d" % r
        axr, rr = v["axr" + tag], v["rr" + tag]

        def zero(ref, i):
            ref[i] = jnp.zeros(ref.shape[1:], F32)

        if LEVEL_OF[r] is FINE:
            when(jnp.logical_not(has_down), functools.partial(zero, axr, 0))
            when(jnp.logical_not(has_up), functools.partial(zero, axr, 1))
        else:
            when(jnp.logical_and(core == 0, x == 0), functools.partial(zero, axr, 0))
            when(jnp.logical_and(core == 1, x == nx - 1), functools.partial(zero, axr, 3))
        when(jnp.logical_not(has_south), functools.partial(zero, rr, 0))
        when(jnp.logical_not(has_north), functools.partial(zero, rr, 1))
    part_s, part_r = v["part_s"], v["part_r"]
    when(jnp.logical_not(has_down), lambda: zero(part_r, 0))
    when(jnp.logical_not(has_up), lambda: zero(part_r, 1))

    def planes(lv, body, lo=0, hi=None, step=1):
        hi = lv.np if hi is None else hi
        for s in range(lv.subs):

            def go(a, carry, s=s):
                a = lo + a * step
                body(s * lv.np + a, s * lv.pad + 1 + a)
                return carry

            lax.fori_loop(0, (hi - lo + step - 1) // step, go, 0)

    def coefficients(lv, tag):
        c, sr, si = v["c" + tag], v["sr" + tag], v["si" + tag]

        def body(sp, carry):
            s = c[25 * lv.sp + sp, 0 : lv.nr, :]
            for i in range(5):
                d = c[6 * i * lv.sp + sp, 0 : lv.nr, :]
                denom = d * d + s * s
                inv = 0.7 / jnp.where(denom > 0, denom, 1.0)
                sr[i * lv.sp + sp, 0 : lv.nr, :] = d * inv
                si[i * lv.sp + sp, 0 : lv.nr, :] = s * inv
            return carry

        lax.fori_loop(0, lv.sp, body, 0)

    def smooth(lv, tag, sp, res):
        sr, si = v["sr" + tag], v["si" + tag]
        new = [None] * 10
        for i in range(5):
            a, b = sr[i * lv.sp + sp, 0 : lv.nr, :], si[i * lv.sp + sp, 0 : lv.nr, :]
            new[i] = a * res[i] + b * res[5 + i]
            new[5 + i] = a * res[5 + i] - b * res[i]
        return new

    def first(lv, tag, u):
        step = first_plane(lv, tag, u)
        planes(lv, lambda sp, pp: step(sp, pp) and None)

    def first_plane(lv, tag, u):
        f = v["f" + tag]

        def step(sp, pp):
            new = smooth(lv, tag, sp, [f[k * lv.sp + sp, 0 : lv.nr, :] for k in range(10)])
            for k in range(10):
                u[k * lv.npl + pp, 8 : 8 + lv.nr, :] = new[k]
            return new

        return step

    def packing(lv):
        return tuple(jnp.zeros((lv.nr, W), F32) for _ in range(lv.packs))

    def pack_plane(lv, xs, sp, r, carry):
        rs = v["rs_%d" % r]
        d, nr = lv.dup, lv.nr
        group = lanes(nr) // (2 * d)
        packed = list(carry)
        for k in range(10):
            slot, j = (k % lv.per) * lv.sp + sp, k // lv.per
            packed[j] = jnp.where(group == slot, roll(xs[k], d + 2 * d * slot), packed[j])
        faces = xs if lv is FINE else [join(xs[k], xs[5 + k]) for k in range(5)]
        for k, w in enumerate(faces):
            rs[0, sp, k : k + 1, :] = w[0:1, :]
            rs[1, sp, k : k + 1, :] = w[nr - 1 : nr, :]
        return tuple(packed)

    def pack_inplane(lv, u, r, step=None):
        ps = v["ps_%d" % r]
        carry = packing(lv)
        for s in range(lv.subs):

            def body(a, carry, s=s):
                sp, pp = s * lv.np + a, s * lv.pad + 1 + a
                if step is None:
                    xs = [u[k * lv.npl + pp, 8 : 8 + lv.nr, :] for k in range(10)]
                else:
                    xs = step(sp, pp)
                return pack_plane(lv, xs, sp, r, carry)

            carry = lax.fori_loop(0, lv.np, body, carry, unroll=UNROLL if lv is not FINE else 2)
        for j in range(lv.packs):
            ps[j, 0 : lv.nr, :] = carry[j]

    def inplane_msgs(lv, r):
        tag = "_%d" % r
        rs, rr, ps, pr = (v[n + tag] for n in ("rs", "rr", "ps", "pr"))
        e, w = (east, west) if lv is FINE else (z_east, z_west)
        return [
            Msg(ps, pr.at[0], e),
            Msg(ps, pr.at[1], w),
            Msg(rs.at[1], rr.at[0], north, has_north, has_south),
            Msg(rs.at[0], rr.at[1], south, has_south, has_north),
        ]

    def pack_axial(lv, u, r):
        axs = v["axs_%d" % r]
        nr = lv.nr
        if lv is FINE:

            def body(k, carry):
                axs[0, k] = u[k * lv.npl + 1, 8 : 8 + nr, :]
                axs[1, k] = u[k * lv.npl + lv.np, 8 : 8 + nr, :]
                return carry

            lax.fori_loop(0, 10, body, 0)
            return
        for q in range(4):
            pp = (q // 2) * lv.pad + (1 if q % 2 == 0 else lv.np)
            for k in range(5):
                axs[q, k, 0:nr, :] = join(
                    u[k * lv.npl + pp, 8 : 8 + nr, :], u[(5 + k) * lv.npl + pp, 8 : 8 + nr, :]
                )

    def axial_msgs(lv, r):
        axs, axr = v["axs_%d" % r], v["axr_%d" % r]
        if lv is FINE:
            return [
                Msg(axs.at[1], axr.at[0], up, has_up, has_down),
                Msg(axs.at[0], axr.at[1], down, has_down, has_up),
            ]
        return [
            Msg(axs.at[3 * core], axr.at[3 - 3 * core], hop, has_hop, has_hop, landing=axr.at[3 * core]),
            Msg(axs.at[pl.ds(1 - core, 3)], axr.at[pl.ds(core, 3)], sibling, landing=axr.at[pl.ds(1 - core, 3)]),
        ]

    def turn(lv, r):
        pr, m = v["pr_%d" % r], v["m_%d" % r]
        d, nr = lv.dup, lv.nr
        low = (lanes(nr) & (2 * d - 1)) < d
        for j in range(lv.packs):
            m[j, 0:nr, :] = jnp.where(low, roll(pr[1, j, 0:nr, :], W - d), roll(pr[0, j, 0:nr, :], d))

    def side_halo(lv, r):
        m = v["m_%d" % r]
        d = lv.dup
        return lambda k, sp: roll(m[k // lv.per, 0 : lv.nr, :], W - d - 2 * d * ((k % lv.per) * lv.sp + sp))

    def row_halo(lv, r, sp):
        rr = v["rr_%d" % r]
        if lv is FINE:
            return [(rr[0, sp, k : k + 1, :], rr[1, sp, k : k + 1, :]) for k in range(10)]
        lo, hi = split(rr[0, sp]), split(rr[1, sp])
        return [(lo[k // 5][k % 5 : k % 5 + 1, :], hi[k // 5][k % 5 : k % 5 + 1, :]) for k in range(10)]

    def ring(nr, d, side, lo, hi):
        lane, row = lanes(nr), lax.broadcasted_iota(jnp.int32, (nr, W), 0)
        h = jnp.where((lane < d) | (lane >= W - d), side, 0.0)
        lo, hi = jnp.broadcast_to(lo, (nr, W)), jnp.broadcast_to(hi, (nr, W))
        return h + jnp.where(row == 0, lo, jnp.where(row == nr - 1, hi, 0.0))

    def inplane(lv, r, sp):
        side = side_halo(lv, r)
        rows = row_halo(lv, r, sp)
        return [ring(lv.nr, lv.dup, side(k, sp), *rows[k]) for k in range(10)]

    def beside(lv, r, q):
        axr = v["axr_%d" % r]
        if lv is FINE:
            return [axr[q, k] for k in range(10)]
        both = [split(axr[q, k, 0 : lv.nr, :]) for k in range(5)]
        return [w[0] for w in both] + [w[1] for w in both]

    def add(lv, tag, u, sp, pp, h):
        corr = smooth(lv, tag, sp, h)
        new = []
        for k in range(10):
            b = k * lv.npl + pp
            new.append(u[b, 8 : 8 + lv.nr, :] + corr[k])
            u[b, 8 : 8 + lv.nr, :] = new[k]
        return new

    def add_axial(lv, tag, u, r):
        for q in range(2 * lv.subs):
            a = 0 if q % 2 == 0 else lv.np - 1
            s = q // 2
            add(lv, tag, u, s * lv.np + a, s * lv.pad + 1 + a, beside(lv, r, q))

    def residual(lv, tag, u, sp, pp):
        f, c = v["f" + tag], v["c" + tag]
        d, nr = lv.dup, lv.nr
        lane = lanes(nr)
        xs, res = [], []
        for k in range(10):
            b = k * lv.npl + pp
            c0 = u[b, 8 : 8 + nr, :]
            y = f[k * lv.sp + sp, 0:nr, :] + (u[b + 1, 8 : 8 + nr, :] + u[b - 1, 8 : 8 + nr, :])
            y = y + (u[b, 7 : 7 + nr, :] + u[b, 9 : 9 + nr, :])
            y = y + (jnp.where(lane < d, 0.0, roll(c0, d)) + jnp.where(lane >= W - d, 0.0, roll(c0, W - d)))
            xs.append(c0)
            res.append(y)
        s = c[25 * lv.sp + sp, 0:nr, :]
        for i in range(5):
            re, im = res[i] + s * xs[5 + i], res[5 + i] - s * xs[i]
            for j in range(5):
                a = c[(5 * i + j) * lv.sp + sp, 0:nr, :]
                re = re - a * xs[j]
                im = im - a * xs[5 + j]
            res[i], res[5 + i] = re, im
        return xs, res

    def interior(lv, tag, u, new):
        def body(sp, pp):
            xs, res = residual(lv, tag, u, sp, pp)
            corr = smooth(lv, tag, sp, res)
            for k in range(10):
                new[k * lv.npl + pp, 8 : 8 + lv.nr, :] = xs[k] + corr[k]

        planes(lv, body)

    t = v["t"]

    def fold(lv, k, y):
        d, nr = lv.dup, lv.nr
        y = y + jnp.where((lanes(nr) & d) == 0, roll(y, W - d), roll(y, d))
        t[k, 0:nr, :] = y
        return t[k, pl.ds(0, nr // 2, stride=2), :] + t[k, pl.ds(1, nr // 2, stride=2), :]

    def send(lv, u, r, step=None):
        pack_inplane(lv, u, r, step)
        b = inplane_msgs(lv, r)
        for msg in b:
            msg.start()
        pack_axial(lv, u, r)
        a = axial_msgs(lv, r)
        for msg in a:
            msg.start()
        return a, b

    def recv(msgs):
        for msg in msgs:
            msg.recv()

    def finish(lv, tag, u, r, after=None):
        a, b = flying.pop(r)
        recv(a)
        add_axial(lv, tag, u, r)
        recv(b)
        turn(lv, r)
        step = lambda sp, pp: add(lv, tag, u, sp, pp, inplane(lv, r, sp))
        if after is None:
            planes(lv, lambda sp, pp: step(sp, pp) and None)
        else:
            flying[after] = send(lv, u, after, step)

    flying = {}
    ua, ub = v["ua0"], v["ub0"]
    f1, c1, c2 = v["f1"], v["c1"], v["c2"]

    for c in loads[:7]:
        c.wait()
    coefficients(FINE, "0")
    first(FINE, "0", ua)

    pack_axial(FINE, ua, 0)
    count = sum(jnp.int32(1) if cond is None else cond.astype(jnp.int32) for _, cond in greet)
    pl.semaphore_wait(barrier, count)
    a0 = axial_msgs(FINE, 0)
    for msg in a0:
        msg.start()
    pack_inplane(FINE, ua, 0)
    b0 = inplane_msgs(FINE, 0)
    for msg in b0:
        msg.start()

    for tag, lv in (("0", FINE), ("1", MID), ("2", COARSE)):
        for u in (v["ua" + tag], v["ub" + tag]):

            def clear(k, carry, u=u, lv=lv):
                for q in range(lv.npl):
                    i = k * lv.npl + q
                    if q % lv.pad in (0, lv.pad - 1):
                        u[i] = jnp.zeros((lv.height, W), F32)
                    else:
                        u[i, 0:8, :] = jnp.zeros((8, W), F32)
                        u[i, 8 + lv.nr : lv.height, :] = jnp.zeros((lv.height - 8 - lv.nr, W), F32)
                return carry

            lax.fori_loop(0, 10, clear, 0)

    for c in loads[7:]:
        c.wait()

    def spread(cells_in):
        count, _, n = cells_in.shape
        pick = (
            lax.broadcasted_iota(jnp.int32, (n, W), 1) // (W // n) == lax.broadcasted_iota(jnp.int32, (n, W), 0)
        ).astype(F32)
        y = jnp.dot(
            cells_in.reshape(count * 8, n), pick, precision=lax.Precision.HIGHEST, preferred_element_type=F32
        )
        return y.reshape(count, 8, W)

    j1, j2, j2p = v["j1"], v["j2"], v["j2p"]
    c1s, c1r, c2s, c2r = v["c1s"], v["c1r"], v["c2s"], v["c2r"]

    def spread1(e, carry):
        y0, y1 = spread(j1[pl.ds(e * 4, 4)]), spread(j1[pl.ds((e + 13) * 4, 4)])
        c1[pl.ds(e * 8 + zh * 4, 4)] = y0
        c1[pl.ds((e + 13) * 8 + zh * 4, 4)] = y1
        for a in range(4):
            c1s[e * 4 + a] = join(y0[a], y1[a])
        return carry

    lax.fori_loop(0, 13, spread1, 0, unroll=13)

    def place2(e, carry):
        j2p[e, 0:4, :] = j2[2 * e]
        j2p[e, 4:8, :] = j2[2 * e + 1]
        return carry

    lax.fori_loop(0, 26, place2, 0, unroll=2)
    y2 = spread(j2p[...])
    for e in range(26):
        c2[e * 4 + zh * 2, 0:4, :] = y2[e, 0:4]
        c2[e * 4 + zh * 2 + 1, 0:4, :] = y2[e, 4:8]
    for e in range(7):
        c2s[e] = join2(join(y2[e], y2[e + 7]), join(y2[e + 14], y2[min(e + 21, 25)]))
    first_part, rest = pl.ds(0, SPLIT), pl.ds(SPLIT, 52 - SPLIT)
    mc = [
        Msg(c1s.at[first_part], c1r.at[first_part], twin),
        Msg(c1s.at[rest], c1r.at[rest], twin),
        Msg(c2s, c2r, twin),
    ]
    interior(FINE, "0", ua, ub)

    recv(b0)
    mc[0].start()
    turn(FINE, 0)
    planes(FINE, lambda sp, pp: add(FINE, "0", ub, sp, pp, inplane(FINE, 0, sp)) and None)
    recv(a0)
    add_axial(FINE, "0", ub, 0)

    for end in range(2):
        for k in range(5):
            pp = 1 if end == 0 else FINE.np
            part_s[end, k] = join(
                fold(FINE, k, ub[k * FINE.npl + pp, 8:24, :]),
                fold(FINE, 5 + k, ub[(5 + k) * FINE.npl + pp, 8:24, :]),
            )
    parts = [
        Msg(part_s.at[1], part_r.at[0], up, has_up, has_down),
        Msg(part_s.at[0], part_r.at[1], down, has_down, has_up),
    ]
    for msg in parts:
        msg.start()
    pack_inplane(FINE, ub, 1)
    b1 = inplane_msgs(FINE, 1)
    for msg in b1:
        msg.start()
    for msg in mc[1:]:
        msg.start()
    f_part = v["f_part"]

    def restrict0(a, carry):
        _, r0 = residual(FINE, "0", ub, 2 * a, 2 * a + 1)
        _, r1 = residual(FINE, "0", ub, 2 * a + 1, 2 * a + 2)
        for k in range(10):
            f_part[k * 4 + a] = 0.125 * fold(FINE, k, r0[k] + r1[k])
        return carry

    lax.fori_loop(0, 4, restrict0, 0)
    recv(b1)
    turn(FINE, 1)

    def restrict_halo0(a, carry):
        h0, h1 = inplane(FINE, 1, 2 * a), inplane(FINE, 1, 2 * a + 1)
        for k in range(10):
            f_part[k * 4 + a] = f_part[k * 4 + a] + 0.125 * fold(FINE, k, h0[k] + h1[k])
        return carry

    lax.fori_loop(0, 4, restrict_halo0, 0)
    gs, gr = v["gs"], v["gr"]
    order = (1, 2, 0, 3)
    mg = [Msg(gs.at[half], gr.at[half], twin) for half in (pl.ds(0, 10), pl.ds(10, 10))]
    for i in range(10):
        k, a = i % 5, order[i // 5]
        gs[i] = join(f_part[k * 4 + a], f_part[(5 + k) * 4 + a])
    mg[0].start()
    recv(parts)
    for k in range(5):
        for end, a in ((0, 0), (1, 3)):
            re, im = split(part_r[end, k])
            f_part[k * 4 + a] = f_part[k * 4 + a] + 0.125 * re
            f_part[(5 + k) * 4 + a] = f_part[(5 + k) * 4 + a] + 0.125 * im
    for i in range(10, 20):
        k, a = i % 5, order[i // 5]
        gs[i] = join(f_part[k * 4 + a], f_part[(5 + k) * 4 + a])
    mg[1].start()
    pack_axial(FINE, ub, 1)
    for k in range(10):
        f1[pl.ds(k * 8 + zh * 4, 4)] = f_part[k * 4 : k * 4 + 4]
    recv(mc)

    def split1(e, carry):
        for a in range(4):
            lo, hi = split(c1r[e * 4 + a])
            c1[e * 8 + (1 - zh) * 4 + a] = lo
            c1[(e + 13) * 8 + (1 - zh) * 4 + a] = hi
        return carry

    lax.fori_loop(0, 13, split1, 0, unroll=2)
    for e in range(7):
        low, high = split2(c2r[e])
        for i, y in enumerate(split(low) + split(high)):
            if e + 7 * i < 26:
                for a in range(2):
                    c2[(e + 7 * i) * 4 + (1 - zh) * 2 + a, 0:4, :] = y[4 * a : 4 * a + 4]
    coefficients(MID, "1")
    coefficients(COARSE, "2")
    recv(mg)
    for i in range(20):
        re, im = split(gr[i])
        k, a = i % 5, order[i // 5]
        f1[k * 8 + (1 - zh) * 4 + a] = re
        f1[(k + 5) * 8 + (1 - zh) * 4 + a] = im

    m_a, m_b = v["ua1"], v["ub1"]
    flying[2] = send(MID, m_a, 2, first_plane(MID, "1", m_a))
    axs1, axr1 = v["axs_1"], v["axr_1"]
    a1 = []

    def piece():
        two = pl.ds(len(a1), 2)
        for dst, dev, there, here in ((0, up, has_up, has_down), (1, down, has_down, has_up)):
            msg = Msg(axs1.at[1 - dst, two], axr1.at[dst, two], dev, there, here)
            msg.start()
            a1.append(msg)

    piece()
    interior(MID, "1", m_a, m_b)
    finish(MID, "1", m_b, 2, 3)
    piece()
    f2 = v["f2"]
    for s in range(2):

        def restrict1(a, carry, s=s):
            _, r0 = residual(MID, "1", m_b, s * 4 + 2 * a, s * 6 + 2 * a + 1)
            _, r1 = residual(MID, "1", m_b, s * 4 + 2 * a + 1, s * 6 + 2 * a + 2)
            for k in range(10):
                f2[k * 4 + s * 2 + a, 0:4, :] = 0.125 * fold(MID, k, r0[k] + r1[k])
            return carry

        lax.fori_loop(0, 2, restrict1, 0)
    a3, b3 = flying.pop(3)
    recv(a3)
    recv(b3)
    turn(MID, 3)
    for s in range(2):
        for a in range(2):
            sp = s * 4 + 2 * a
            h0, h1, h2 = inplane(MID, 3, sp), inplane(MID, 3, sp + 1), beside(MID, 3, 2 * s + a)
            for k in range(10):
                i = k * 4 + s * 2 + a
                f2[i, 0:4, :] = f2[i, 0:4, :] + 0.125 * fold(MID, k, h0[k] + h1[k] + h2[k])

    q_a, q_b = v["ua2"], v["ub2"]
    flying[4] = send(COARSE, q_a, 4, first_plane(COARSE, "2", q_a))
    for r in range(4, 3 + COARSE_SWEEPS):
        piece()
        interior(COARSE, "2", q_a, q_b)
        finish(COARSE, "2", q_b, r, r + 1 if r < 2 + COARSE_SWEEPS else None)
        q_a, q_b = q_b, q_a

    def prolong1(sp, pp):
        s, a = sp // 4, lax.rem(sp, 4)
        xs = []
        for k in range(10):
            w = q_a[k * COARSE.npl + s * 4 + 1 + a // 2, 8:16, :]
            t[k, pl.ds(0, 8, stride=2), :] = w
            t[k, pl.ds(1, 8, stride=2), :] = w
            b = k * MID.npl + pp
            xs.append(m_b[b, 8:16, :] + t[k, 0:8, :])
            m_b[b, 8:16, :] = xs[k]
        return xs

    flying[7] = send(MID, m_b, 7, prolong1)
    interior(MID, "1", m_b, m_a)
    finish(MID, "1", m_a, 7, 8)
    interior(MID, "1", m_a, m_b)
    finish(MID, "1", m_b, 8, 9)

    def double(k, w):
        t[k, pl.ds(0, 8, stride=2), :] = w
        t[k, pl.ds(1, 8, stride=2), :] = w
        return t[k, 0:16, :]

    def prolong0(a, carry):
        for k in range(10):
            w = m_b[k * MID.npl + zh * 6 + 1 + a // 2, 8:16, :]
            b = k * FINE.npl + 1 + a
            ub[b, 8:24, :] = ub[b, 8:24, :] + double(k, w)
        return carry

    lax.fori_loop(0, 8, prolong0, 0)
    interior(FINE, "0", ub, ua)
    planes(FINE, lambda sp, pp: add(FINE, "0", ua, sp, pp, inplane(FINE, 1, sp)) and None)
    recv(a1)
    add_axial(FINE, "0", ua, 1)
    a9, b9 = flying.pop(9)
    recv(a9)
    axr9 = v["axr_9"]
    for end, a in ((0, 0), (1, 7)):
        both = [split(axr9[2 * zh + end, k]) for k in range(5)]
        h = [w[0] for w in both] + [w[1] for w in both]
        add(FINE, "0", ua, a, a + 1, [double(k, h[k]) for k in range(10)])
    recv(b9)
    turn(MID, 9)
    side9 = side_halo(MID, 9)

    def add9(sp, pp):
        am = zh * 4 + sp // 2
        rows = row_halo(MID, 9, am)
        return add(FINE, "0", ua, sp, pp, [ring(16, 1, double(k, side9(k, am)), *rows[k]) for k in range(10)])

    planes(FINE, lambda sp, pp: add9(sp, pp) and None, 0, 8, 7)
    pack_axial(FINE, ua, 10)
    a10 = axial_msgs(FINE, 10)
    for msg in a10:
        msg.start()
    planes(FINE, lambda sp, pp: add9(sp, pp) and None, 1, 7)
    pack_inplane(FINE, ua, 10)
    b10 = inplane_msgs(FINE, 10)
    for msg in b10:
        msg.start()

    mask = v["mask"]
    interior(FINE, "0", ua, ub)
    recv(b10)
    turn(FINE, 10)

    def work(a, new):
        for k in range(10):
            out[k * 8 + a] = new[k]
        return mask[a].astype(F32) * (new[4] * new[6] - new[9] * new[1])

    def last(a, acc):
        return acc + work(a, add(FINE, "0", ub, a, a + 1, inplane(FINE, 10, a)))

    acc = lax.fori_loop(1, 7, last, jnp.zeros((16, W), F32))
    planes(FINE, lambda sp, pp: add(FINE, "0", ub, sp, pp, inplane(FINE, 10, sp)) and None, 0, 8, 7)
    recv(a10)
    for end, a in ((0, 0), (1, 7)):
        acc = acc + work(a, add(FINE, "0", ub, a, a + 1, beside(FINE, 10, end)))

    def total(buf, group, value):
        mine, count, members = group
        buf[mine, 0:1] = value
        row = pl.ds(0, 1)
        msgs = [
            Msg(buf.at[mine, row], buf.at[mine, row], dev, landing=buf.at[slot, row]) for dev, slot in members
        ]
        earlier = list(sent)
        sent.clear()
        for msg in msgs:
            msg.start()
        for msg in earlier:
            when(msg.send_if, msg.copy.wait_send)
        recv(msgs)
        parts = [buf[i, 0:1] for i in range(count)]
        while len(parts) > 1:
            parts = [p + q for p, q in zip(parts[::2], parts[1::2])] + parts[len(parts) - len(parts) % 2 :]
        return parts[0]

    def offsets(*counts):
        far = lambda o: sum(min(d, n - d) for d, n in zip(o, counts))
        every = [(i, j) for i in range(counts[0]) for j in range(counts[1])]
        return sorted(every[1:], key=lambda o: -far(o))

    across = []
    for i, j in offsets(nx, n_rad):
        there = lambda sign: (lax.rem(x + sign * i + nx, nx), lax.rem(rad + sign * j + n_rad, n_rad))
        (tx, ty), (fx, fy) = there(1), there(-1)
        across.append((place(tx, ty, z, core), fx * n_rad + fy))
    along = []
    for i, j in offsets(nz, 2):
        tz, fz = lax.rem(z + i, nz), lax.rem(z + nz - i, nz)
        other = core if j == 0 else 1 - core
        along.append((place(x, rad, tz, other), fz * 2 + other))
    sum_xy = total(v["red0"], (x * n_rad + rad, nx * n_rad, across), jnp.sum(acc, axis=0, keepdims=True))
    sum_all = total(v["red1"], (z * 2 + core, nz * 2, along), sum_xy)
    damp[0, 0] = jnp.sum(sum_all) * (25.0 / jnp.sqrt(jnp.float32(cells)))
    for msg in sent:
        when(msg.send_if, msg.copy.wait_send)


def solution(mesh):
    sizes = (mesh.shape["axial"], mesh.shape["radial"], mesh.shape["pitch"])

    def on_device(rhs, jac0, shift0, jac1, shift1, jac2, shift2, blade_mask):
        cells = shift0.size * sizes[0] * sizes[1] * sizes[2]
        shapes = scratch()
        out, damp = pl.pallas_call(
            functools.partial(kernel, sizes + (cells,), tuple(shapes)),
            out_shape=(jax.ShapeDtypeStruct((80, 16, W), F32), jax.ShapeDtypeStruct((1, 1), F32)),
            in_specs=[pl.BlockSpec(memory_space=pltpu.HBM)] * 8,
            out_specs=(pl.BlockSpec(memory_space=pltpu.VMEM), pl.BlockSpec(memory_space=pltpu.SMEM)),
            scratch_shapes=list(shapes.values()),
            compiler_params=pltpu.CompilerParams(
                collective_id=0, has_side_effects=True, vmem_limit_bytes=48 * 1024 * 1024
            ),
        )(
            *(
                pltpu.with_memory_space_constraint(a, pltpu.HBM)
                for a in (
                    rhs.reshape(80, 16, W),
                    jac0.reshape(200, 16, W),
                    shift0,
                    jac1.reshape(100, 8, 64),
                    shift1,
                    jac2.reshape(50, 4, 32),
                    shift2,
                    blade_mask,
                )
            )
        )
        return out.reshape(rhs.shape), damp.reshape(())

    spec = P(None, None, "axial", "radial", "pitch")
    flat = P("axial", "radial", "pitch")
    return jax.shard_map(
        on_device,
        mesh=mesh,
        in_specs=(spec, spec, flat, spec, flat, spec, flat, flat),
        out_specs=(spec, P()),
        check_vma=False,
    )
```

```python
import functools

import jax
import jax.numpy as jnp
from jax import lax
from jax.experimental import pallas as pl
from jax.experimental.pallas import tpu as pltpu
from jax.sharding import PartitionSpec as P

COARSE_SWEEPS = 4
MESH = pl.DeviceIdType.MESH
W = 128
F32 = jnp.float32


class Level:
    def __init__(self, rows, planes, subs, dup):
        self.nr, self.np, self.subs, self.dup = rows, planes, subs, dup
        self.sp = planes * subs
        self.pad = planes + 2
        self.npl = self.pad * subs
        self.nr8 = max(rows, 8)
        self.height = self.nr8 + 16
        self.per = 64 // (dup * self.sp)
        self.packs = -(-10 // self.per)


FINE = Level(16, 8, 1, 1)
MID = Level(8, 4, 2, 2)
COARSE = Level(4, 2, 2, 4)


def lanes(rows):
    return lax.broadcasted_iota(jnp.int32, (rows, W), 1)


def roll(x, shift):
    return pltpu.roll(x, shift, 1)


def join(a, b):
    return jnp.where((lanes(a.shape[0]) & 1) == 0, a, b)


def split(w):
    even = (lanes(w.shape[0]) & 1) == 0
    return jnp.where(even, w, roll(w, 1)), jnp.where(even, roll(w, W - 1), w)


def join2(a, b):
    return jnp.where((lanes(a.shape[0]) & 2) == 0, a, b)


def split2(w):
    low = (lanes(w.shape[0]) & 2) == 0
    return jnp.where(low, w, roll(w, 2)), jnp.where(low, roll(w, W - 2), w)


def scratch():
    shapes = {}

    def vmem(name, *shape):
        shapes[name] = pltpu.VMEM(shape, F32)

    for tag, lv in (("0", FINE), ("1", MID), ("2", COARSE)):
        vmem("ua" + tag, 10 * lv.npl, lv.height, W)
        vmem("ub" + tag, 10 * lv.npl, lv.height, W)
        vmem("f" + tag, 10 * lv.sp, lv.nr8, W)
        vmem("c" + tag, 26 * lv.sp, lv.nr8, W)
        vmem("sr" + tag, 5 * lv.sp, lv.nr8, W)
        vmem("si" + tag, 5 * lv.sp, lv.nr8, W)
    for r in range(ROUNDS):
        lv = LEVEL_OF[r]
        tag = "_%d" % r
        fields, ends = (10, 2) if lv is FINE else (5, 4)
        vmem("axs" + tag, ends, fields, lv.nr8, W)
        vmem("axr" + tag, ends, fields, lv.nr8, W)
        vmem("rs" + tag, 2, lv.sp, 16 if lv is FINE else 8, W)
        vmem("rr" + tag, 2, lv.sp, 16 if lv is FINE else 8, W)
        vmem("ps" + tag, lv.packs, lv.nr8, W)
        vmem("pr" + tag, 2, lv.packs, lv.nr8, W)
        vmem("m" + tag, lv.packs, lv.nr8, W)
    vmem("part_s", 2, 5, 8, W)
    vmem("part_r", 2, 5, 8, W)
    vmem("f_part", 40, 8, W)
    vmem("gs", 20, 8, W)
    vmem("gr", 20, 8, W)
    vmem("c1s", 52, 8, W)
    vmem("c1r", 52, 8, W)
    vmem("c2s", 7, 8, W)
    vmem("c2r", 7, 8, W)
    vmem("t", 10, 48, W)
    vmem("j1", 104, 8, 64)
    vmem("j2", 52, 4, 32)
    vmem("j2p", 26, 8, 32)
    vmem("red0", 16, 8, W)
    vmem("red1", 16, 8, W)
    shapes["mask"] = pltpu.VMEM((8, 16, W), jnp.int32)
    shapes["ss"] = pltpu.SemaphoreType.DMA((COPIES,))
    shapes["rs"] = pltpu.SemaphoreType.DMA((COPIES,))
    shapes["ls"] = pltpu.SemaphoreType.DMA((16,))
    return shapes


LEVEL_OF = [FINE, FINE, MID, MID, COARSE, COARSE, COARSE, MID, MID, MID, FINE]
ROUNDS = len(LEVEL_OF)
COPIES = 128
UNROLL = 4
SPLIT = 20


def kernel(sizes, names, *refs):
    rhs, jac0, shift0, jac1, shift1, jac2, shift2, blade = refs[:8]
    out, damp = refs[8:10]
    v = dict(zip(names, refs[10:]))
    n_ax, n_rad, n_pit, cells = sizes

    ax, rad, pit = lax.axis_index("axial"), lax.axis_index("radial"), lax.axis_index("pitch")
    core = lax.rem(ax, 2)
    zh = lax.rem(ax // 2, 2)
    x = ax // 4
    nx = n_ax // 4
    z = zh * n_pit + pit
    nz = 2 * n_pit

    def place(xx, yy, zz, cc):
        return {"axial": xx * 4 + (zz // n_pit) * 2 + cc, "radial": yy, "pitch": lax.rem(zz, n_pit)}

    up, down = {"axial": ax + 1}, {"axial": ax - 1}
    has_up, has_down = ax < n_ax - 1, ax > 0
    north, south = {"radial": rad + 1}, {"radial": rad - 1}
    has_north, has_south = rad < n_rad - 1, rad > 0
    east, west = {"pitch": lax.rem(pit + 1, n_pit)}, {"pitch": lax.rem(pit + n_pit - 1, n_pit)}
    z_east, z_west = place(x, rad, lax.rem(z + 1, nz), core), place(x, rad, lax.rem(z + nz - 1, nz), core)
    twin = {"axial": ax + 2 - 4 * zh}
    sibling = {"axial": ax + 1 - 2 * core}
    hop = {"axial": ax + 6 * core - 3}
    has_hop = jnp.logical_or(jnp.logical_and(core == 0, x > 0), jnp.logical_and(core == 1, x < nx - 1))
    wrap_e = pit == n_pit - 1
    wrap_w = pit == 0

    def when(cond, act):
        if cond is None:
            act()
        else:
            pl.when(cond)(act)

    barrier = pltpu.get_barrier_semaphore()
    greet = [
        (up, has_up),
        (down, has_down),
        (north, has_north),
        (south, has_south),
        (east, None),
        (west, None),
        (twin, None),
        (hop, has_hop),
        (z_east, wrap_e),
        (z_west, wrap_w),
    ]
    for dev, cond in greet:
        when(cond, lambda dev=dev: pl.semaphore_signal(barrier, inc=1, device_id=dev, device_id_type=MESH))

    local = [
        (rhs, v["f0"]),
        (shift0, v["c0"].at[pl.ds(200, 8)]),
        *((jac0.at[pl.ds(48 * i, 8)], v["c0"].at[pl.ds(48 * i, 8)]) for i in range(5)),
        *((jac0.at[pl.ds(48 * i + 8, 40)], v["c0"].at[pl.ds(48 * i + 8, 40)]) for i in range(4)),
        (jac1, v["j1"].at[pl.ds(0, 100)]),
        (shift1, v["j1"].at[pl.ds(100, 4)]),
        (jac2, v["j2"].at[pl.ds(0, 50)]),
        (shift2, v["j2"].at[pl.ds(50, 2)]),
        (blade, v["mask"]),
    ]
    loads = [pltpu.make_async_copy(a, b, v["ls"].at[i]) for i, (a, b) in enumerate(local)]
    for c in loads:
        c.start()

    counter = [0]
    sent = []

    class Msg:
        def __init__(self, src, dst, dev, send_if=None, recv_if=None, landing=None):
            i = counter[0]
            counter[0] += 1
            make = lambda d: pltpu.make_async_remote_copy(
                src_ref=src, dst_ref=d, send_sem=v["ss"].at[i], recv_sem=v["rs"].at[i], device_id=dev, device_id_type=MESH
            )
            self.copy = make(dst)
            self.into = self.copy if landing is None else make(landing)
            self.send_if, self.recv_if = send_if, recv_if

        def start(self):
            when(self.send_if, self.copy.start)
            sent.append(self)

        def recv(self):
            when(self.recv_if, self.into.wait_recv)

    for r in range(ROUNDS):
        tag = "_%d" % r
        axr, rr = v["axr" + tag], v["rr" + tag]

        def zero(ref, i):
            ref[i] = jnp.zeros(ref.shape[1:], F32)

        if LEVEL_OF[r] is FINE:
            when(jnp.logical_not(has_down), functools.partial(zero, axr, 0))
            when(jnp.logical_not(has_up), functools.partial(zero, axr, 1))
        else:
            when(jnp.logical_and(core == 0, x == 0), functools.partial(zero, axr, 0))
            when(jnp.logical_and(core == 1, x == nx - 1), functools.partial(zero, axr, 3))
        when(jnp.logical_not(has_south), functools.partial(zero, rr, 0))
        when(jnp.logical_not(has_north), functools.partial(zero, rr, 1))
    part_s, part_r = v["part_s"], v["part_r"]
    when(jnp.logical_not(has_down), lambda: zero(part_r, 0))
    when(jnp.logical_not(has_up), lambda: zero(part_r, 1))

    def planes(lv, body, lo=0, hi=None, step=1):
        hi = lv.np if hi is None else hi
        for s in range(lv.subs):

            def go(a, carry, s=s):
                a = lo + a * step
                body(s * lv.np + a, s * lv.pad + 1 + a)
                return carry

            lax.fori_loop(0, (hi - lo + step - 1) // step, go, 0)

    def coefficients(lv, tag):
        c, sr, si = v["c" + tag], v["sr" + tag], v["si" + tag]

        def body(sp, carry):
            s = c[25 * lv.sp + sp, 0 : lv.nr, :]
            for i in range(5):
                d = c[6 * i * lv.sp + sp, 0 : lv.nr, :]
                denom = d * d + s * s
                inv = 0.7 / jnp.where(denom > 0, denom, 1.0)
                sr[i * lv.sp + sp, 0 : lv.nr, :] = d * inv
                si[i * lv.sp + sp, 0 : lv.nr, :] = s * inv
            return carry

        lax.fori_loop(0, lv.sp, body, 0)

    def smooth(lv, tag, sp, res):
        sr, si = v["sr" + tag], v["si" + tag]
        new = [None] * 10
        for i in range(5):
            a, b = sr[i * lv.sp + sp, 0 : lv.nr, :], si[i * lv.sp + sp, 0 : lv.nr, :]
            new[i] = a * res[i] + b * res[5 + i]
            new[5 + i] = a * res[5 + i] - b * res[i]
        return new

    def first(lv, tag, u):
        step = first_plane(lv, tag, u)
        planes(lv, lambda sp, pp: step(sp, pp) and None)

    def first_plane(lv, tag, u):
        f = v["f" + tag]

        def step(sp, pp):
            new = smooth(lv, tag, sp, [f[k * lv.sp + sp, 0 : lv.nr, :] for k in range(10)])
            for k in range(10):
                u[k * lv.npl + pp, 8 : 8 + lv.nr, :] = new[k]
            return new

        return step

    def packing(lv):
        return tuple(jnp.zeros((lv.nr, W), F32) for _ in range(lv.packs))

    def pack_plane(lv, xs, sp, r, carry):
        rs = v["rs_%d" % r]
        d, nr = lv.dup, lv.nr
        group = lanes(nr) // (2 * d)
        packed = list(carry)
        for k in range(10):
            slot, j = (k % lv.per) * lv.sp + sp, k // lv.per
            packed[j] = jnp.where(group == slot, roll(xs[k], d + 2 * d * slot), packed[j])
        faces = xs if lv is FINE else [join(xs[k], xs[5 + k]) for k in range(5)]
        for k, w in enumerate(faces):
            rs[0, sp, k : k + 1, :] = w[0:1, :]
            rs[1, sp, k : k + 1, :] = w[nr - 1 : nr, :]
        return tuple(packed)

    def pack_inplane(lv, u, r, step=None):
        ps = v["ps_%d" % r]
        carry = packing(lv)
        for s in range(lv.subs):

            def body(a, carry, s=s):
                sp, pp = s * lv.np + a, s * lv.pad + 1 + a
                if step is None:
                    xs = [u[k * lv.npl + pp, 8 : 8 + lv.nr, :] for k in range(10)]
                else:
                    xs = step(sp, pp)
                return pack_plane(lv, xs, sp, r, carry)

            carry = lax.fori_loop(0, lv.np, body, carry, unroll=UNROLL if lv is not FINE else 2)
        for j in range(lv.packs):
            ps[j, 0 : lv.nr, :] = carry[j]

    def inplane_msgs(lv, r):
        tag = "_%d" % r
        rs, rr, ps, pr = (v[n + tag] for n in ("rs", "rr", "ps", "pr"))
        e, w = (east, west) if lv is FINE else (z_east, z_west)
        return [
            Msg(ps, pr.at[0], e),
            Msg(ps, pr.at[1], w),
            Msg(rs.at[1], rr.at[0], north, has_north, has_south),
            Msg(rs.at[0], rr.at[1], south, has_south, has_north),
        ]

    def pack_axial(lv, u, r):
        axs = v["axs_%d" % r]
        nr = lv.nr
        if lv is FINE:

            def body(k, carry):
                axs[0, k] = u[k * lv.npl + 1, 8 : 8 + nr, :]
                axs[1, k] = u[k * lv.npl + lv.np, 8 : 8 + nr, :]
                return carry

            lax.fori_loop(0, 10, body, 0)
            return
        for q in range(4):
            pp = (q // 2) * lv.pad + (1 if q % 2 == 0 else lv.np)
            for k in range(5):
                axs[q, k, 0:nr, :] = join(
                    u[k * lv.npl + pp, 8 : 8 + nr, :], u[(5 + k) * lv.npl + pp, 8 : 8 + nr, :]
                )

    def axial_msgs(lv, r):
        axs, axr = v["axs_%d" % r], v["axr_%d" % r]
        if lv is FINE:
            return [
                Msg(axs.at[1], axr.at[0], up, has_up, has_down),
                Msg(axs.at[0], axr.at[1], down, has_down, has_up),
            ]
        return [
            Msg(axs.at[3 * core], axr.at[3 - 3 * core], hop, has_hop, has_hop, landing=axr.at[3 * core]),
            Msg(axs.at[pl.ds(1 - core, 3)], axr.at[pl.ds(core, 3)], sibling, landing=axr.at[pl.ds(1 - core, 3)]),
        ]

    def turn(lv, r):
        pr, m = v["pr_%d" % r], v["m_%d" % r]
        d, nr = lv.dup, lv.nr
        low = (lanes(nr) & (2 * d - 1)) < d
        for j in range(lv.packs):
            m[j, 0:nr, :] = jnp.where(low, roll(pr[1, j, 0:nr, :], W - d), roll(pr[0, j, 0:nr, :], d))

    def side_halo(lv, r):
        m = v["m_%d" % r]
        d = lv.dup
        return lambda k, sp: roll(m[k // lv.per, 0 : lv.nr, :], W - d - 2 * d * ((k % lv.per) * lv.sp + sp))

    def row_halo(lv, r, sp):
        rr = v["rr_%d" % r]
        if lv is FINE:
            return [(rr[0, sp, k : k + 1, :], rr[1, sp, k : k + 1, :]) for k in range(10)]
        lo, hi = split(rr[0, sp]), split(rr[1, sp])
        return [(lo[k // 5][k % 5 : k % 5 + 1, :], hi[k // 5][k % 5 : k % 5 + 1, :]) for k in range(10)]

    def ring(nr, d, side, lo, hi):
        lane, row = lanes(nr), lax.broadcasted_iota(jnp.int32, (nr, W), 0)
        h = jnp.where((lane < d) | (lane >= W - d), side, 0.0)
        lo, hi = jnp.broadcast_to(lo, (nr, W)), jnp.broadcast_to(hi, (nr, W))
        return h + jnp.where(row == 0, lo, jnp.where(row == nr - 1, hi, 0.0))

    def inplane(lv, r, sp):
        side = side_halo(lv, r)
        rows = row_halo(lv, r, sp)
        return [ring(lv.nr, lv.dup, side(k, sp), *rows[k]) for k in range(10)]

    def beside(lv, r, q):
        axr = v["axr_%d" % r]
        if lv is FINE:
            return [axr[q, k] for k in range(10)]
        both = [split(axr[q, k, 0 : lv.nr, :]) for k in range(5)]
        return [w[0] for w in both] + [w[1] for w in both]

    def add(lv, tag, u, sp, pp, h):
        corr = smooth(lv, tag, sp, h)
        new = []
        for k in range(10):
            b = k * lv.npl + pp
            new.append(u[b, 8 : 8 + lv.nr, :] + corr[k])
            u[b, 8 : 8 + lv.nr, :] = new[k]
        return new

    def add_axial(lv, tag, u, r):
        for q in range(2 * lv.subs):
            a = 0 if q % 2 == 0 else lv.np - 1
            s = q // 2
            add(lv, tag, u, s * lv.np + a, s * lv.pad + 1 + a, beside(lv, r, q))

    def residual(lv, tag, u, sp, pp):
        f, c = v["f" + tag], v["c" + tag]
        d, nr = lv.dup, lv.nr
        lane = lanes(nr)
        xs, res = [], []
        for k in range(10):
            b = k * lv.npl + pp
            c0 = u[b, 8 : 8 + nr, :]
            y = f[k * lv.sp + sp, 0:nr, :] + (u[b + 1, 8 : 8 + nr, :] + u[b - 1, 8 : 8 + nr, :])
            y = y + (u[b, 7 : 7 + nr, :] + u[b, 9 : 9 + nr, :])
            y = y + (jnp.where(lane < d, 0.0, roll(c0, d)) + jnp.where(lane >= W - d, 0.0, roll(c0, W - d)))
            xs.append(c0)
            res.append(y)
        s = c[25 * lv.sp + sp, 0:nr, :]
        for i in range(5):
            re, im = res[i] + s * xs[5 + i], res[5 + i] - s * xs[i]
            for j in range(5):
                a = c[(5 * i + j) * lv.sp + sp, 0:nr, :]
                re = re - a * xs[j]
                im = im - a * xs[5 + j]
            res[i], res[5 + i] = re, im
        return xs, res

    def interior(lv, tag, u, new):
        def body(sp, pp):
            xs, res = residual(lv, tag, u, sp, pp)
            corr = smooth(lv, tag, sp, res)
            for k in range(10):
                new[k * lv.npl + pp, 8 : 8 + lv.nr, :] = xs[k] + corr[k]

        planes(lv, body)

    t = v["t"]

    def fold(lv, k, y):
        d, nr = lv.dup, lv.nr
        y = y + jnp.where((lanes(nr) & d) == 0, roll(y, W - d), roll(y, d))
        t[k, 0:nr, :] = y
        return t[k, pl.ds(0, nr // 2, stride=2), :] + t[k, pl.ds(1, nr // 2, stride=2), :]

    def send(lv, u, r, step=None):
        pack_inplane(lv, u, r, step)
        b = inplane_msgs(lv, r)
        for msg in b:
            msg.start()
        pack_axial(lv, u, r)
        a = axial_msgs(lv, r)
        for msg in a:
            msg.start()
        return a, b

    def recv(msgs):
        for msg in msgs:
            msg.recv()

    def finish(lv, tag, u, r, after=None):
        a, b = flying.pop(r)
        recv(a)
        add_axial(lv, tag, u, r)
        recv(b)
        turn(lv, r)
        step = lambda sp, pp: add(lv, tag, u, sp, pp, inplane(lv, r, sp))
        if after is None:
            planes(lv, lambda sp, pp: step(sp, pp) and None)
        else:
            flying[after] = send(lv, u, after, step)

    flying = {}
    ua, ub = v["ua0"], v["ub0"]
    f1, c1, c2 = v["f1"], v["c1"], v["c2"]

    for c in loads[:7]:
        c.wait()
    coefficients(FINE, "0")
    first(FINE, "0", ua)

    pack_axial(FINE, ua, 0)
    count = sum(jnp.int32(1) if cond is None else cond.astype(jnp.int32) for _, cond in greet)
    pl.semaphore_wait(barrier, count)
    a0 = axial_msgs(FINE, 0)
    for msg in a0:
        msg.start()
    pack_inplane(FINE, ua, 0)
    b0 = inplane_msgs(FINE, 0)
    for msg in b0:
        msg.start()

    for tag, lv in (("0", FINE), ("1", MID), ("2", COARSE)):
        for u in (v["ua" + tag], v["ub" + tag]):

            def clear(k, carry, u=u, lv=lv):
                for q in range(lv.npl):
                    i = k * lv.npl + q
                    if q % lv.pad in (0, lv.pad - 1):
                        u[i] = jnp.zeros((lv.height, W), F32)
                    else:
                        u[i, 0:8, :] = jnp.zeros((8, W), F32)
                        u[i, 8 + lv.nr : lv.height, :] = jnp.zeros((lv.height - 8 - lv.nr, W), F32)
                return carry

            lax.fori_loop(0, 10, clear, 0)

    for c in loads[7:]:
        c.wait()

    def spread(cells_in):
        count, _, n = cells_in.shape
        pick = (
            lax.broadcasted_iota(jnp.int32, (n, W), 1) // (W // n) == lax.broadcasted_iota(jnp.int32, (n, W), 0)
        ).astype(F32)
        y = jnp.dot(
            cells_in.reshape(count * 8, n), pick, precision=lax.Precision.HIGHEST, preferred_element_type=F32
        )
        return y.reshape(count, 8, W)

    j1, j2, j2p = v["j1"], v["j2"], v["j2p"]
    c1s, c1r, c2s, c2r = v["c1s"], v["c1r"], v["c2s"], v["c2r"]

    def spread1(e, carry):
        y0, y1 = spread(j1[pl.ds(e * 4, 4)]), spread(j1[pl.ds((e + 13) * 4, 4)])
        c1[pl.ds(e * 8 + zh * 4, 4)] = y0
        c1[pl.ds((e + 13) * 8 + zh * 4, 4)] = y1
        for a in range(4):
            c1s[e * 4 + a] = join(y0[a], y1[a])
        return carry

    lax.fori_loop(0, 13, spread1, 0, unroll=13)

    def place2(e, carry):
        j2p[e, 0:4, :] = j2[2 * e]
        j2p[e, 4:8, :] = j2[2 * e + 1]
        return carry

    lax.fori_loop(0, 26, place2, 0, unroll=2)
    y2 = spread(j2p[...])
    for e in range(26):
        c2[e * 4 + zh * 2, 0:4, :] = y2[e, 0:4]
        c2[e * 4 + zh * 2 + 1, 0:4, :] = y2[e, 4:8]
    for e in range(7):
        c2s[e] = join2(join(y2[e], y2[e + 7]), join(y2[e + 14], y2[min(e + 21, 25)]))
    first_part, rest = pl.ds(0, SPLIT), pl.ds(SPLIT, 52 - SPLIT)
    mc = [
        Msg(c1s.at[first_part], c1r.at[first_part], twin),
        Msg(c1s.at[rest], c1r.at[rest], twin),
        Msg(c2s, c2r, twin),
    ]
    interior(FINE, "0", ua, ub)

    recv(b0)
    mc[0].start()
    turn(FINE, 0)
    planes(FINE, lambda sp, pp: add(FINE, "0", ub, sp, pp, inplane(FINE, 0, sp)) and None)
    recv(a0)
    add_axial(FINE, "0", ub, 0)

    for end in range(2):
        for k in range(5):
            pp = 1 if end == 0 else FINE.np
            part_s[end, k] = join(
                fold(FINE, k, ub[k * FINE.npl + pp, 8:24, :]),
                fold(FINE, 5 + k, ub[(5 + k) * FINE.npl + pp, 8:24, :]),
            )
    parts = [
        Msg(part_s.at[1], part_r.at[0], up, has_up, has_down),
        Msg(part_s.at[0], part_r.at[1], down, has_down, has_up),
    ]
    for msg in parts:
        msg.start()
    pack_inplane(FINE, ub, 1)
    b1 = inplane_msgs(FINE, 1)
    for msg in b1:
        msg.start()
    for msg in mc[1:]:
        msg.start()
    f_part = v["f_part"]

    def restrict0(a, carry):
        _, r0 = residual(FINE, "0", ub, 2 * a, 2 * a + 1)
        _, r1 = residual(FINE, "0", ub, 2 * a + 1, 2 * a + 2)
        for k in range(10):
            f_part[k * 4 + a] = 0.125 * fold(FINE, k, r0[k] + r1[k])
        return carry

    lax.fori_loop(0, 4, restrict0, 0)
    recv(b1)
    turn(FINE, 1)

    def restrict_halo0(a, carry):
        h0, h1 = inplane(FINE, 1, 2 * a), inplane(FINE, 1, 2 * a + 1)
        for k in range(10):
            f_part[k * 4 + a] = f_part[k * 4 + a] + 0.125 * fold(FINE, k, h0[k] + h1[k])
        return carry

    lax.fori_loop(0, 4, restrict_halo0, 0)
    gs, gr = v["gs"], v["gr"]
    order = (1, 2, 0, 3)
    mg = [Msg(gs.at[half], gr.at[half], twin) for half in (pl.ds(0, 10), pl.ds(10, 10))]
    for i in range(10):
        k, a = i % 5, order[i // 5]
        gs[i] = join(f_part[k * 4 + a], f_part[(5 + k) * 4 + a])
    mg[0].start()
    recv(parts)
    for k in range(5):
        for end, a in ((0, 0), (1, 3)):
            re, im = split(part_r[end, k])
            f_part[k * 4 + a] = f_part[k * 4 + a] + 0.125 * re
            f_part[(5 + k) * 4 + a] = f_part[(5 + k) * 4 + a] + 0.125 * im
    for i in range(10, 20):
        k, a = i % 5, order[i // 5]
        gs[i] = join(f_part[k * 4 + a], f_part[(5 + k) * 4 + a])
    mg[1].start()
    pack_axial(FINE, ub, 1)
    for k in range(10):
        f1[pl.ds(k * 8 + zh * 4, 4)] = f_part[k * 4 : k * 4 + 4]
    recv(mc)

    def split1(e, carry):
        for a in range(4):
            lo, hi = split(c1r[e * 4 + a])
            c1[e * 8 + (1 - zh) * 4 + a] = lo
            c1[(e + 13) * 8 + (1 - zh) * 4 + a] = hi
        return carry

    lax.fori_loop(0, 13, split1, 0, unroll=2)
    for e in range(7):
        low, high = split2(c2r[e])
        for i, y in enumerate(split(low) + split(high)):
            if e + 7 * i < 26:
                for a in range(2):
                    c2[(e + 7 * i) * 4 + (1 - zh) * 2 + a, 0:4, :] = y[4 * a : 4 * a + 4]
    coefficients(MID, "1")
    coefficients(COARSE, "2")
    recv(mg)
    for i in range(20):
        re, im = split(gr[i])
        k, a = i % 5, order[i // 5]
        f1[k * 8 + (1 - zh) * 4 + a] = re
        f1[(k + 5) * 8 + (1 - zh) * 4 + a] = im

    m_a, m_b = v["ua1"], v["ub1"]
    flying[2] = send(MID, m_a, 2, first_plane(MID, "1", m_a))
    axs1, axr1 = v["axs_1"], v["axr_1"]
    a1 = []

    def piece():
        two = pl.ds(len(a1), 2)
        for dst, dev, there, here in ((0, up, has_up, has_down), (1, down, has_down, has_up)):
            msg = Msg(axs1.at[1 - dst, two], axr1.at[dst, two], dev, there, here)
            msg.start()
            a1.append(msg)

    piece()
    interior(MID, "1", m_a, m_b)
    finish(MID, "1", m_b, 2, 3)
    piece()
    f2 = v["f2"]
    for s in range(2):

        def restrict1(a, carry, s=s):
            _, r0 = residual(MID, "1", m_b, s * 4 + 2 * a, s * 6 + 2 * a + 1)
            _, r1 = residual(MID, "1", m_b, s * 4 + 2 * a + 1, s * 6 + 2 * a + 2)
            for k in range(10):
                f2[k * 4 + s * 2 + a, 0:4, :] = 0.125 * fold(MID, k, r0[k] + r1[k])
            return carry

        lax.fori_loop(0, 2, restrict1, 0)
    a3, b3 = flying.pop(3)
    recv(a3)
    recv(b3)
    turn(MID, 3)
    for s in range(2):
        for a in range(2):
            sp = s * 4 + 2 * a
            h0, h1, h2 = inplane(MID, 3, sp), inplane(MID, 3, sp + 1), beside(MID, 3, 2 * s + a)
            for k in range(10):
                i = k * 4 + s * 2 + a
                f2[i, 0:4, :] = f2[i, 0:4, :] + 0.125 * fold(MID, k, h0[k] + h1[k] + h2[k])

    q_a, q_b = v["ua2"], v["ub2"]
    flying[4] = send(COARSE, q_a, 4, first_plane(COARSE, "2", q_a))
    for r in range(4, 3 + COARSE_SWEEPS):
        piece()
        interior(COARSE, "2", q_a, q_b)
        finish(COARSE, "2", q_b, r, r + 1 if r < 2 + COARSE_SWEEPS else None)
        q_a, q_b = q_b, q_a

    def prolong1(sp, pp):
        s, a = sp // 4, lax.rem(sp, 4)
        xs = []
        for k in range(10):
            w = q_a[k * COARSE.npl + s * 4 + 1 + a // 2, 8:16, :]
            t[k, pl.ds(0, 8, stride=2), :] = w
            t[k, pl.ds(1, 8, stride=2), :] = w
            b = k * MID.npl + pp
            xs.append(m_b[b, 8:16, :] + t[k, 0:8, :])
            m_b[b, 8:16, :] = xs[k]
        return xs

    flying[7] = send(MID, m_b, 7, prolong1)
    interior(MID, "1", m_b, m_a)
    finish(MID, "1", m_a, 7, 8)
    interior(MID, "1", m_a, m_b)
    finish(MID, "1", m_b, 8, 9)

    def double(k, w):
        t[k, pl.ds(0, 8, stride=2), :] = w
        t[k, pl.ds(1, 8, stride=2), :] = w
        return t[k, 0:16, :]

    def prolong0(a, carry):
        for k in range(10):
            w = m_b[k * MID.npl + zh * 6 + 1 + a // 2, 8:16, :]
            b = k * FINE.npl + 1 + a
            ub[b, 8:24, :] = ub[b, 8:24, :] + double(k, w)
        return carry

    lax.fori_loop(0, 8, prolong0, 0)
    interior(FINE, "0", ub, ua)
    planes(FINE, lambda sp, pp: add(FINE, "0", ua, sp, pp, inplane(FINE, 1, sp)) and None)
    recv(a1)
    add_axial(FINE, "0", ua, 1)
    a9, b9 = flying.pop(9)
    recv(a9)
    axr9 = v["axr_9"]
    for end, a in ((0, 0), (1, 7)):
        both = [split(axr9[2 * zh + end, k]) for k in range(5)]
        h = [w[0] for w in both] + [w[1] for w in both]
        add(FINE, "0", ua, a, a + 1, [double(k, h[k]) for k in range(10)])
    recv(b9)
    turn(MID, 9)
    side9 = side_halo(MID, 9)

    def add9(sp, pp):
        am = zh * 4 + sp // 2
        rows = row_halo(MID, 9, am)
        return add(FINE, "0", ua, sp, pp, [ring(16, 1, double(k, side9(k, am)), *rows[k]) for k in range(10)])

    planes(FINE, lambda sp, pp: add9(sp, pp) and None, 0, 8, 7)
    pack_axial(FINE, ua, 10)
    a10 = axial_msgs(FINE, 10)
    for msg in a10:
        msg.start()
    planes(FINE, lambda sp, pp: add9(sp, pp) and None, 1, 7)
    pack_inplane(FINE, ua, 10)
    b10 = inplane_msgs(FINE, 10)
    for msg in b10:
        msg.start()

    mask = v["mask"]
    interior(FINE, "0", ua, ub)
    recv(b10)
    turn(FINE, 10)

    def work(a, new):
        for k in range(10):
            out[k * 8 + a] = new[k]
        return mask[a].astype(F32) * (new[4] * new[6] - new[9] * new[1])

    def last(a, acc):
        return acc + work(a, add(FINE, "0", ub, a, a + 1, inplane(FINE, 10, a)))

    acc = lax.fori_loop(1, 7, last, jnp.zeros((16, W), F32))
    planes(FINE, lambda sp, pp: add(FINE, "0", ub, sp, pp, inplane(FINE, 10, sp)) and None, 0, 8, 7)
    recv(a10)
    for end, a in ((0, 0), (1, 7)):
        acc = acc + work(a, add(FINE, "0", ub, a, a + 1, beside(FINE, 10, end)))

    def total(buf, group, value):
        mine, count, members = group
        buf[mine, 0:1] = value
        row = pl.ds(0, 1)
        msgs = [
            Msg(buf.at[mine, row], buf.at[mine, row], dev, landing=buf.at[slot, row]) for dev, slot in members
        ]
        earlier = list(sent)
        sent.clear()
        for msg in msgs:
            msg.start()
        for msg in earlier:
            when(msg.send_if, msg.copy.wait_send)
        recv(msgs)
        parts = [buf[i, 0:1] for i in range(count)]
        while len(parts) > 1:
            parts = [p + q for p, q in zip(parts[::2], parts[1::2])] + parts[len(parts) - len(parts) % 2 :]
        return parts[0]

    def offsets(*counts):
        far = lambda o: sum(min(d, n - d) for d, n in zip(o, counts))
        every = [(i, j) for i in range(counts[0]) for j in range(counts[1])]
        return sorted(every[1:], key=lambda o: -far(o))

    across = []
    for i, j in offsets(nx, n_rad):
        there = lambda sign: (lax.rem(x + sign * i + nx, nx), lax.rem(rad + sign * j + n_rad, n_rad))
        (tx, ty), (fx, fy) = there(1), there(-1)
        across.append((place(tx, ty, z, core), fx * n_rad + fy))
    along = []
    for i, j in offsets(nz, 2):
        tz, fz = lax.rem(z + i, nz), lax.rem(z + nz - i, nz)
        other = core if j == 0 else 1 - core
        along.append((place(x, rad, tz, other), fz * 2 + other))
    sum_xy = total(v["red0"], (x * n_rad + rad, nx * n_rad, across), jnp.sum(acc, axis=0, keepdims=True))
    sum_all = total(v["red1"], (z * 2 + core, nz * 2, along), sum_xy)
    damp[0, 0] = jnp.sum(sum_all) * (25.0 / jnp.sqrt(jnp.float32(cells)))
    for msg in sent:
        when(msg.send_if, msg.copy.wait_send)


def solution(mesh):
    sizes = (mesh.shape["axial"], mesh.shape["radial"], mesh.shape["pitch"])

    def on_device(rhs, jac0, shift0, jac1, shift1, jac2, shift2, blade_mask):
        cells = shift0.size * sizes[0] * sizes[1] * sizes[2]
        shapes = scratch()
        out, damp = pl.pallas_call(
            functools.partial(kernel, sizes + (cells,), tuple(shapes)),
            out_shape=(jax.ShapeDtypeStruct((80, 16, W), F32), jax.ShapeDtypeStruct((1, 1), F32)),
            in_specs=[pl.BlockSpec(memory_space=pltpu.HBM)] * 8,
            out_specs=(pl.BlockSpec(memory_space=pltpu.VMEM), pl.BlockSpec(memory_space=pltpu.SMEM)),
            scratch_shapes=list(shapes.values()),
            compiler_params=pltpu.CompilerParams(
                collective_id=0, has_side_effects=True, vmem_limit_bytes=48 * 1024 * 1024
            ),
        )(
            *(
                pltpu.with_memory_space_constraint(a, pltpu.HBM)
                for a in (
                    rhs.reshape(80, 16, W),
                    jac0.reshape(200, 16, W),
                    shift0,
                    jac1.reshape(100, 8, 64),
                    shift1,
                    jac2.reshape(50, 4, 32),
                    shift2,
                    blade_mask,
                )
            )
        )
        return out.reshape(rhs.shape), damp.reshape(())

    spec = P(None, None, "axial", "radial", "pitch")
    flat = P("axial", "radial", "pitch")
    return jax.shard_map(
        on_device,
        mesh=mesh,
        in_specs=(spec, spec, flat, spec, flat, spec, flat, flat),
        out_specs=(spec, P()),
        check_vma=False,
    )
```
